32 devices in a mesh: dom: 8 (over y, x, core), sub: 4 (over z).
Axes of the slice: x: 2, y: 2, z: 4, core: 2. Of those that a mesh axis runs over, the one named last changes fastest.
Arguments:
- adjoint_rhs: float32 [384, 320], P(('dom', 'sub')), may hold values from -6 to 6
- adjoint_start: float32 [384, 320], P(('dom', 'sub')), may hold values from -6 to 6
- offdiag_blocks: bfloat16 [6, 384, 320, 320], P(None, ('dom', 'sub')), may hold values from -0.125 to 0.125
- diag_inverse: float32 [384, 320, 320], P(('dom', 'sub')), may hold values from -0.3125 to 0.3125
- geometry_jac: bfloat16 [384, 24, 320], P(('dom', 'sub')), may hold values from -0.125 to 0.125
- neighbor: int32 [384, 6], P(('dom', 'sub')), may hold values from -1 to 383, as said below
- corner_node: int32 [384, 8], P(('dom', 'sub')), may hold values from 0 to 566, as said below
- deform_place: int32 [567], replicated, may hold values from 0 to 575, as said below
- stiff_diag: float32 [3, 3, 576], P(None, None, ('dom', 'sub')), may hold values from -3.5 to 3.5
- stiff_upper: float32 [3, 3, 576], P(None, None, ('dom', 'sub')), may hold values from -3.5 to 3.5
- stiff_lower: float32 [3, 3, 576], P(None, None, ('dom', 'sub')), may hold values from -3.5 to 3.5
Outputs:
- adjoint: float32 [384, 320], P(('dom', 'sub'))
- shape_grad: float32 [3, 576], P(None, ('dom', 'sub'))
The draws below stay inside these ranges and needn't reach their ends.
Inputs may be any that keep to these rules, and one draw needn't show every extreme that they name: Elements are numbered device by device in the order of dom then sub, 12 to a device. The relation is symmetric: neighbor[e, k] = f >= 0 implies neighbor[f, k xor 1] = e. A neighbour across face 0 or 1 lies on the same device or on the device one step up (face 0) or down (face 1) along dom with the same sub index; across face 2 or 3 on the same device or one step up (face 2) or down (face 3) along sub; across faces 4 and 5 on the same device. At most 12 faces 0 of one device, and as many faces 1, lead to another device, and at most 6 faces 2, and as many faces 3; these counts are reached. `corner_node`: elements that share a corner name the same node. `deform_place`: the positions are distinct.
All inputs are finite; a program needn't handle non-finite values.
Results may differ from the reference program's by a relative error of at most 0.0042.
Values sent between devices are 32-bit elements; how exact they have to be, the bound alone decides.
No kernel may reach another device: no remote copies, remote signals or barrier semaphores. Data moves between devices by JAX's collectives and lax.ppermute only.
A program may use at most 128 MiB of HBM per device.

```python
import jax
import jax.numpy as jnp
from jax import lax

NB = 320
NF = 6
BX = 1
BY = 2
BZ = 6
SWEEPS = 2
E_DEV = 12
ELEMENTS = 384
GNODES = 567
NODES = 576
N_DOM = 8
N_SUB = 4


def local_orders(key):
    devices = N_DOM * N_SUB
    keys = jax.random.split(jax.random.fold_in(key, 7), devices)

    def one_order(order_key):
        return jax.random.permutation(order_key, E_DEV).astype(jnp.int32)
    position = jax.vmap(one_order)(keys)
    rows = jnp.arange(devices, dtype=jnp.int32)[:, None]
    numbers = jnp.broadcast_to(jnp.arange(E_DEV, dtype=jnp.int32)[None, :], (devices, E_DEV))
    element_of = jnp.zeros((devices, E_DEV), jnp.int32).at[rows, position].set(numbers)
    return (position, element_of)


def element_coords(position):
    devices = N_DOM * N_SUB
    owner = jnp.repeat(jnp.arange(devices, dtype=jnp.int32), E_DEV)
    place = position.reshape(-1)
    grid_x = owner // N_SUB * BX + place // (BY * BZ)
    grid_y = owner % N_SUB * BY + place // BZ % BY
    grid_z = place % BZ
    return (grid_x, grid_y, grid_z)


def draw_neighbor(key, part):
    position, element_of = local_orders(key)
    grid_x, grid_y, grid_z = element_coords(position)
    columns_out = []
    for step_x, step_y, step_z in ((1, 0, 0), (-1, 0, 0), (0, 1, 0), (0, -1, 0), (0, 0, 1), (0, 0, -1)):
        next_x = grid_x + step_x
        next_y = grid_y + step_y
        next_z = grid_z + step_z
        inside = (next_x >= 0) & (next_x < N_DOM * BX) & (next_y >= 0) & (next_y < N_SUB * BY) & (next_z >= 0) & (next_z < BZ)
        clip_x = jnp.clip(next_x, 0, N_DOM * BX - 1)
        clip_y = jnp.clip(next_y, 0, N_SUB * BY - 1)
        clip_z = jnp.clip(next_z, 0, BZ - 1)
        owner = clip_x // BX * N_SUB + clip_y // BY
        place = clip_x % BX * (BY * BZ) + clip_y % BY * BZ + clip_z
        element_id = owner * E_DEV + element_of[owner, place]
        columns_out.append(jnp.where(inside, element_id, -1))
    return jnp.stack(columns_out, 1).astype(jnp.int32)


def draw_corner_node(key, part):
    position, element_of = local_orders(key)
    grid_x, grid_y, grid_z = element_coords(position)
    span_y = N_SUB * BY + 1
    columns_out = []
    for corner in range(8):
        shift_x = corner // 4
        shift_y = corner // 2 % 2
        shift_z = corner % 2
        node_id = ((grid_x + shift_x) * span_y + grid_y + shift_y) * (BZ + 1) + grid_z + shift_z
        columns_out.append(node_id)
    return jnp.stack(columns_out, 1).astype(jnp.int32)


def draw_deform_place(key, part):
    order = jax.random.permutation(jax.random.fold_in(key, 11), NODES).astype(jnp.int32)
    chosen = order[:GNODES]
    chosen = jnp.where(jnp.max(chosen) < NODES - 1, chosen.at[0].set(NODES - 1), chosen)
    chosen = jnp.where(jnp.min(chosen) > 0, chosen.at[1].set(0), chosen)
    return chosen.astype(jnp.int32)


def block_levels(own_key, shape, cuts, least, largest):
    level = 1.0
    for axis_at, blocks in cuts:
        heights = jax.random.uniform(jax.random.fold_in(jax.random.fold_in(own_key, 6), axis_at), (blocks,), jnp.float32, least / len(cuts), largest / len(cuts))
        level = level * jnp.repeat(jnp.exp(heights), shape[axis_at] // blocks).reshape((-1,) + (1,) * (len(shape) - 1 - axis_at))
    return level


def centred(own_key, extent, width, most, cuts=(), kind=jnp.bfloat16):
    factor_of = block_levels(own_key, extent, cuts, -0.22, 0.18) if cuts else 1.0
    drawn = jax.random.normal(own_key, extent, jnp.float32) * width * factor_of
    return jnp.minimum(jnp.maximum(drawn, -most), most).astype(kind)


def setup_inputs(seed: int = 0) -> dict:
    seeds = jax.random.split(jax.random.key(seed), 12)
    adjoint_rhs = centred(seeds[0], (ELEMENTS, NB), 1.0, 6.0, ((0, 32),), jnp.float32)
    adjoint_start = centred(seeds[1], (ELEMENTS, NB), 1.0, 6.0, ((0, 32),), jnp.float32)
    offdiag_blocks = centred(seeds[2], (NF, ELEMENTS, NB, NB), (6 * NB) ** -0.5, 0.125, ((1, 32),))
    diag_inverse = centred(seeds[3], (ELEMENTS, NB, NB), NB ** -0.5, 0.3125, ((0, 32),), jnp.float32)
    geometry_jac = centred(seeds[4], (ELEMENTS, 24, NB), (8 * NB) ** -0.5, 0.125, ((0, 32),))
    neighbor = draw_neighbor(jax.random.fold_in(seeds[11], 71), 0)
    corner_node = draw_corner_node(jax.random.fold_in(seeds[11], 71), 0)
    deform_place = draw_deform_place(jax.random.fold_in(seeds[11], 71), 0)
    stiff_diag = centred(seeds[8], (3, 3, NODES), 3 ** -0.5, 3.5, ((2, 32),), jnp.float32)
    stiff_upper = centred(seeds[9], (3, 3, NODES), 3 ** -0.5, 3.5, ((2, 32),), jnp.float32)
    stiff_lower = centred(seeds[10], (3, 3, NODES), 3 ** -0.5, 3.5, ((2, 32),), jnp.float32)
    return {"adjoint_rhs": adjoint_rhs, "adjoint_start": adjoint_start, "offdiag_blocks": offdiag_blocks, "diag_inverse": diag_inverse, "geometry_jac": geometry_jac, "neighbor": neighbor, "corner_node": corner_node, "deform_place": deform_place, "stiff_diag": stiff_diag, "stiff_upper": stiff_upper, "stiff_lower": stiff_lower}


precise = lax.Precision.HIGHEST


def reference(adjoint_rhs, adjoint_start, offdiag_blocks, diag_inverse, geometry_jac, neighbor, corner_node, deform_place, stiff_diag, stiff_upper, stiff_lower):
    elem_count = adjoint_rhs.shape[0]
    groups = elem_count // E_DEV
    has_face = neighbor >= 0
    target = jnp.where(has_face, neighbor, elem_count).astype(jnp.int32)
    adjoint = adjoint_start
    for sweep_index in range(SWEEPS):
        rounded = lax.optimization_barrier(adjoint.astype(jnp.bfloat16)).astype(jnp.float32)

        def face_block(group_index):
            start = (group_index * E_DEV).astype(jnp.int32)
            blocks = lax.dynamic_slice_in_dim(offdiag_blocks, start, E_DEV, 1).astype(jnp.float32)
            piece = lax.dynamic_slice_in_dim(rounded, start, E_DEV, 0)
            return jnp.einsum("keij,ei->kej", blocks, piece, precision=precise)

        terms = lax.map(face_block, jnp.arange(groups, dtype=jnp.int32))
        terms = terms.transpose(1, 0, 2, 3).reshape(NF, elem_count, NB)
        carried = jnp.zeros((elem_count + 1, NB), jnp.float32)
        for face_index in range(NF):
            carried = carried.at[target[:, face_index]].add(terms[face_index])
        carried = carried[:elem_count]
        adjoint = jnp.einsum("eij,ej->ei", diag_inverse, adjoint_rhs - carried, precision=precise)
    rounded = lax.optimization_barrier(adjoint.astype(jnp.bfloat16)).astype(jnp.float32)
    corner_terms = jnp.einsum("emi,ei->em", geometry_jac.astype(jnp.float32), rounded, precision=precise)
    places = deform_place[corner_node.reshape(-1)].astype(jnp.int32)
    values = corner_terms.reshape(elem_count, 8, 3).transpose(2, 0, 1).reshape(3, 8 * elem_count)
    node_sens = jnp.zeros((3, NODES), jnp.float32).at[:, places].add(values)
    upper_term = jnp.einsum("abq,aq->bq", stiff_upper, node_sens, precision=precise)
    zero_column = jnp.zeros((3, 1), jnp.float32)
    prev_term = jnp.concatenate([zero_column, upper_term[:, :-1]], 1)
    next_sens = jnp.concatenate([node_sens[:, 1:], zero_column], 1)
    shape_grad = jnp.einsum("abq,aq->bq", stiff_diag, node_sens, precision=precise) + prev_term
    shape_grad = shape_grad + jnp.einsum("abq,aq->bq", stiff_lower, next_sens, precision=precise)
    return adjoint, shape_grad
```

```python
import jax
import jax.numpy as jnp
from jax import lax
from jax.experimental import pallas as pl
from jax.experimental.pallas import tpu as pltpu
from jax.sharding import PartitionSpec as P

NF = 6
CORNERS = 8
AXES = ("dom", "sub")
ROWS = 16

f32 = jnp.float32
bf16 = jnp.bfloat16
i32 = jnp.int32

IN_HBM = pl.BlockSpec(memory_space=pltpu.HBM)
IN_VMEM = pl.BlockSpec(memory_space=pltpu.VMEM)


def iota(shape, dim):
    return lax.broadcasted_iota(i32, shape, dim)


def up_to(count, multiple):
    return -(-count // multiple) * multiple


def in_three(value):
    first = value.astype(bf16)
    rest = value - first.astype(f32)
    second = rest.astype(bf16)
    return first, second, (rest - second.astype(f32)).astype(bf16)


def one_hot_dot(chooser, value):
    return sum(jnp.dot(chooser, part, preferred_element_type=f32) for part in in_three(value))


def dot_nt(a, b):
    return lax.dot_general(a, b, (((1,), (1,)), ((), ())), preferred_element_type=f32)


def pair_swaps(n_dom, n_sub):
    def at(d, s):
        return d * n_sub + s

    swaps = []
    for first in (0, 1):
        pairs = []
        for s in range(n_sub):
            for d in range(first, n_dom - 1, 2):
                pairs += [(at(d, s), at(d + 1, s)), (at(d + 1, s), at(d, s))]
        swaps.append(pairs)
    for first in (0, 1):
        pairs = []
        for d in range(n_dom):
            for s in range(first, n_sub - 1, 2):
                pairs += [(at(d, s), at(d, s + 1)), (at(d, s + 1), at(d, s))]
        swaps.append(pairs)
    for index in (1, 3):
        used = {source for source, _ in swaps[index]}
        for d in range(n_dom):
            for s in range(n_sub):
                other = (d, s ^ 1) if index == 1 else (d ^ 1, s)
                if at(d, s) in used or other[0] >= n_dom or other[1] >= n_sub:
                    continue
                if at(*other) not in used:
                    swaps[index].append((at(d, s), at(*other)))
    return swaps


def face_products(elem_count, adj_rows, blocks, faces, before=None):
    def one_element(e, _):
        if before is not None:
            before(e)
        row = adj_rows[pl.ds(e, 1), :].astype(bf16)
        for k in range(NF):
            faces[k, pl.ds(e, 1), :] = jnp.dot(row, blocks[k, e], preferred_element_type=f32)
        return 0

    lax.fori_loop(0, elem_count, one_element, 0)


def fill_sends(faces, sends):
    dom_even = lax.axis_index("dom") % 2 == 0
    sub_even = lax.axis_index("sub") % 2 == 0
    sends[0][...] = jnp.where(dom_even, faces[0], faces[1])
    sends[1][...] = jnp.where(dom_even, faces[1], faces[0])
    sends[2][...] = jnp.where(sub_even, faces[2], faces[3])
    sends[3][...] = jnp.where(sub_even, faces[3], faces[2])


def sum_chooser(elem_count, n_sub, neighbor_rows, square):
    dom, sub = lax.axis_index("dom"), lax.axis_index("sub")
    device = dom * n_sub + sub
    first = device * elem_count
    square[...] = jnp.zeros(square.shape, i32)
    square[0:NF, 0:elem_count] = neighbor_rows
    by_element = square[...].T[0:ROWS, :]
    dom_odd, sub_odd = dom % 2, sub % 2
    slots = (dom_odd, 1 - dom_odd, 2 + sub_odd, 3 - sub_odd)
    offsets = (n_sub, -n_sub, 1, -1)
    columns = iota((ROWS, (NF + 4) * ROWS), 1)
    live = iota((ROWS, 1), 0) < elem_count
    total = jnp.zeros(columns.shape, f32)
    for k in range(NF):
        ids = by_element[:, k : k + 1]
        inside = (ids >= first) & (ids < first + elem_count)
        column = (k ^ 1) * ROWS + ids - first
        if k < 4:
            away = (NF + slots[k]) * ROWS + ids - first - offsets[k] * elem_count
            column = jnp.where(inside, column, away)
        column = jnp.where(live & (ids >= 0), column, -1)
        total = total + jnp.where(columns == column, 1.0, 0.0)
    return total


def corner_lanes(elem_count, node_count, corner_rows, place_row):
    width = 3 * CORNERS * elem_count
    lane = iota((CORNERS, width), 1)
    inner = lane - 3 * CORNERS * jnp.floor((lane.astype(f32) + 0.5) / (3 * CORNERS)).astype(i32)
    mine = inner - 3 * iota((CORNERS, width), 0)
    mine = (mine >= 0) & (mine < 3)
    offset = iota((elem_count, width), 1) - 3 * CORNERS * iota((elem_count, width), 0)
    spread = jnp.where((offset >= 0) & (offset < 3 * CORNERS), 1.0, 0.0).astype(bf16)
    corners = corner_rows.astype(f32)
    high = jnp.floor(corners / 128.0)
    low = corners - 128.0 * high
    nodes = 128.0 * jnp.dot(high.astype(bf16), spread, preferred_element_type=f32)
    nodes = nodes + jnp.dot(low.astype(bf16), spread, preferred_element_type=f32)
    nodes = jnp.sum(jnp.where(mine, nodes, 0.0), axis=0, keepdims=True).astype(i32)
    count = place_row.shape[1]
    found = jnp.where(iota((count, width), 0) == nodes, 1.0, 0.0).astype(bf16)
    place = jnp.broadcast_to(place_row.astype(f32), (8, count))
    owner = jnp.floor((place + 0.5) / node_count)
    slot = place - node_count * owner
    pair = jnp.where(iota((8, count), 0) == 0, owner, slot).astype(bf16)
    return jnp.dot(pair, found, preferred_element_type=f32)


def first_sweep(elem_count, n_sub, node_count, start, offdiag, neighbor, corner, place, upper,
                send_0, send_1, send_2, send_3, faces, blocks, chooser, table,
                start_v, neighbor_v, corner_v, place_v, upper_v, square, small_sem, block_sem):
    sends = (send_0, send_1, send_2, send_3)
    small = [
        pltpu.make_async_copy(source, target, small_sem.at[n])
        for n, (source, target) in enumerate(
            ((start, start_v), (neighbor, neighbor_v), (corner, corner_v), (place, place_v),
             (upper, upper_v))
        )
    ]

    def block_copy(e):
        return pltpu.make_async_copy(offdiag.at[:, e], blocks.at[:, e], block_sem.at[e])

    for copy in small:
        copy.start()
    for e in range(elem_count):
        block_copy(e).start()
    faces[...] = jnp.zeros(faces.shape, f32)
    for copy in small:
        copy.wait()
    chooser[...] = sum_chooser(elem_count, n_sub, neighbor_v[...], square)
    table[...] = jnp.zeros(table.shape, f32)
    width = 3 * CORNERS * elem_count
    table[0:8, 0:width] = corner_lanes(elem_count, node_count, corner_v[...], place_v[...])
    base = 3 * (node_count + 2)
    lane, row = iota((3, 128), 1), iota((3, 128), 0)
    last = jnp.zeros((3, 128), f32)
    for a in range(3):
        column = upper_v[a][:, node_count - 1 : node_count]
        last = last + jnp.where(lane == base + 3 * a + row, column, 0.0)
    table[2:3, 0:128] = jnp.sum(last, axis=0, keepdims=True)
    face_products(elem_count, start_v, blocks, faces, before=lambda e: block_copy(e).wait())
    fill_sends(faces, sends)


def apply_inverse(elem_count, rhs, faces, arrived, chooser, inverse, carried_v, columns):
    size = rhs.shape[1]
    terms = jnp.concatenate(
        [faces[...].reshape(NF * ROWS, size)] + [a[...] for a in arrived], axis=0
    )
    carried = one_hot_dot(chooser[...].astype(bf16), terms)
    carried_v[0:elem_count, :] = rhs[...] - carried[0:elem_count, :]
    lane = iota((size, 128), 1)
    columns[...] = jnp.zeros(columns.shape, f32)

    def one_element(e, _):
        product = inverse[e] * carried_v[pl.ds(e, 1), :]
        total = jnp.sum(product, axis=1, keepdims=True)
        columns[0:size, :] = jnp.where(lane == e, total, columns[0:size, :])
        return 0

    lax.fori_loop(0, elem_count, one_element, 0)
    return columns[...].T[0:ROWS, 0:size]


def next_sweep(elem_count, rhs, faces_in, arr_0, arr_1, arr_2, arr_3, chooser, inverse, blocks,
               send_0, send_1, send_2, send_3, faces, carried_v, columns, adj_v):
    adj_v[...] = apply_inverse(
        elem_count, rhs, faces_in, (arr_0, arr_1, arr_2, arr_3), chooser, inverse, carried_v, columns
    )
    faces[...] = jnp.zeros(faces.shape, f32)
    face_products(elem_count, adj_v, blocks, faces)
    fill_sends(faces, (send_0, send_1, send_2, send_3))


def last_sweep(elem_count, n_sub, n_dev, node_count, rhs, faces_in, arr_0, arr_1, arr_2, arr_3,
               chooser, inverse, geometry, table, adjoint, out, carried_v, columns):
    rows = apply_inverse(
        elem_count, rhs, faces_in, (arr_0, arr_1, arr_2, arr_3), chooser, inverse, carried_v, columns
    )
    adjoint[...] = rows[0:elem_count, :]
    width = 3 * CORNERS * elem_count
    slots = node_count + 2
    every = dot_nt(rows.astype(bf16), geometry[...])
    offset = iota(every.shape, 1) - 3 * CORNERS * iota(every.shape, 0)
    own = (offset >= 0) & (offset < 3 * CORNERS)
    corner = jnp.sum(jnp.where(own, every, 0.0), axis=0, keepdims=True)
    parts = in_three(corner)
    owner = table[0:1, 0:width].astype(i32)
    slot = table[1:2, 0:width].astype(i32)
    lane = iota((1, width), 1)
    third = lane - 3 * jnp.floor((lane.astype(f32) + 0.5) / 3.0).astype(i32)
    is_first, is_last = slot == 0, slot == node_count - 1
    beside = jnp.where(is_first, owner - 1, jnp.where(is_last, owner + 1, -1))
    beside_slot = jnp.where(is_first, slots - 1, 0)
    total = jnp.zeros((n_dev, 128), f32)
    for target, place in ((owner, slot + 1), (beside, beside_slot)):
        goes = iota((n_dev, width), 0) == target
        left = jnp.concatenate(
            [jnp.where(goes, part.astype(f32), 0.0).astype(bf16) for part in parts], axis=0
        )
        right = jnp.where(iota((128, width), 0) == third * slots + place, 1.0, 0.0).astype(bf16)
        summed = dot_nt(left, right)
        total = total + summed[0:n_dev] + summed[n_dev : 2 * n_dev] + summed[2 * n_dev :]
    device = lax.axis_index("dom") * n_sub + lax.axis_index("sub")
    after = iota((n_dev, 128), 0) == device + 1
    out[...] = total + jnp.where(after, table[2:3, 0:128], 0.0)


def stencil(node_count, arrived, diag, upper, lower, out, shifted):
    slots = node_count + 2
    sums = jnp.broadcast_to(jnp.sum(arrived[...], axis=0, keepdims=True), (8, 128))
    lane, row = iota((8, 128), 1), iota((8, 128), 0)

    def at(a, step):
        first = a * slots + 1 + step
        return pltpu.roll(sums, (128 - first) % 128, axis=1)[0:3, 0:node_count]

    total = jnp.zeros((3, node_count), f32)
    moved = jnp.zeros((3, node_count), f32)
    edge = jnp.zeros((8, 1), f32)
    for a in range(3):
        here = at(a, 0)
        total = total + diag[a] * here + lower[a] * at(a, 1)
        moved = moved + upper[a] * here
        coupling = jnp.sum(jnp.where(lane == 3 * slots + 3 * a + row, sums, 0.0), 1, keepdims=True)
        before = jnp.sum(jnp.where(lane == a * slots, sums, 0.0), 1, keepdims=True)
        edge = edge + coupling * before
    shifted[...] = jnp.zeros(shifted.shape, f32)
    shifted[0:3, 0:node_count] = moved
    prev = jnp.where(lane == 0, edge, pltpu.roll(shifted[...], 1, axis=1))
    out[...] = total + prev[0:3, 0:node_count]


def solution(mesh):
    n_dom, n_sub = mesh.shape["dom"], mesh.shape["sub"]
    n_dev = n_dom * n_sub
    swaps = pair_swaps(n_dom, n_sub)

    def exchange(sends):
        return [lax.ppermute(send, AXES, pairs) for send, pairs in zip(sends, swaps)]

    def on_device(
        adjoint_rhs, adjoint_start, offdiag_blocks, diag_inverse, geometry_jac, neighbor,
        corner_node, deform_place, stiff_diag, stiff_upper, stiff_lower,
    ):
        elem_count, size = adjoint_rhs.shape
        node_count = stiff_diag.shape[2]
        assert elem_count <= ROWS and n_dev <= 256 and 1 < node_count <= 256
        assert 3 * (node_count + 2) + 9 <= 128
        width = 3 * CORNERS * elem_count
        slab = jax.ShapeDtypeStruct((ROWS, size), f32)
        faces_shape = jax.ShapeDtypeStruct((NF, ROWS, size), f32)
        limit = pltpu.CompilerParams(vmem_limit_bytes=16 << 20)
        column_scratch = [
            pltpu.VMEM((ROWS, size), f32),
            pltpu.VMEM((up_to(size, 128), 128), f32),
        ]

        def fixed(body, *numbers):
            def call(*refs):
                return body(*numbers, *refs)

            return call

        *sends, faces, blocks, chooser, table = pl.pallas_call(
            fixed(first_sweep, elem_count, n_sub, node_count),
            out_shape=(
                slab, slab, slab, slab, faces_shape,
                pltpu.VMEM(offdiag_blocks.shape, bf16),
                jax.ShapeDtypeStruct((ROWS, (NF + 4) * ROWS), f32),
                jax.ShapeDtypeStruct((8, up_to(width, 128)), f32),
            ),
            in_specs=[IN_HBM] * 6,
            out_specs=(IN_VMEM,) * 8,
            scratch_shapes=[
                pltpu.VMEM((elem_count, size), f32),
                pltpu.VMEM((NF, elem_count), i32),
                pltpu.VMEM((CORNERS, elem_count), i32),
                pltpu.VMEM((1, deform_place.shape[0]), i32),
                pltpu.VMEM(stiff_upper.shape, f32),
                pltpu.VMEM((128, 128), i32),
                pltpu.SemaphoreType.DMA((5,)),
                pltpu.SemaphoreType.DMA((elem_count,)),
            ],
            compiler_params=limit,
            name="first_sweep",
        )(adjoint_start, offdiag_blocks, neighbor.T, corner_node.T, deform_place[None, :],
          stiff_upper)
        diag_inverse, faces = lax.optimization_barrier((diag_inverse, faces))
        inverse = pltpu.with_memory_space_constraint(diag_inverse, pltpu.VMEM)
        arrived = exchange(sends)
        *sends, faces = pl.pallas_call(
            fixed(next_sweep, elem_count),
            out_shape=(slab, slab, slab, slab, faces_shape),
            in_specs=[IN_VMEM] * 9,
            out_specs=(IN_VMEM,) * 5,
            scratch_shapes=column_scratch + [pltpu.VMEM((ROWS, size), f32)],
            compiler_params=limit,
            name="next_sweep",
        )(adjoint_rhs, faces, *arrived, chooser, inverse, blocks)
        arrived = exchange(sends)
        adjoint, by_owner = pl.pallas_call(
            fixed(last_sweep, elem_count, n_sub, n_dev, node_count),
            out_shape=(
                jax.ShapeDtypeStruct((elem_count, size), f32),
                jax.ShapeDtypeStruct((n_dev, 128), f32),
            ),
            in_specs=[IN_VMEM] * 10,
            out_specs=(IN_VMEM,) * 2,
            scratch_shapes=column_scratch,
            compiler_params=limit,
            name="last_sweep",
        )(adjoint_rhs, faces, *arrived, chooser, inverse,
          geometry_jac.reshape(width, size), table)
        gathered = lax.all_to_all(by_owner, AXES, 0, 0, tiled=True)
        shape_grad = pl.pallas_call(
            fixed(stencil, node_count),
            out_shape=jax.ShapeDtypeStruct((3, node_count), f32),
            in_specs=[IN_VMEM] * 4,
            out_specs=IN_VMEM,
            scratch_shapes=[pltpu.VMEM((8, 128), f32)],
            compiler_params=limit,
            name="stencil",
        )(gathered, stiff_diag, stiff_upper, stiff_lower)
        return adjoint, shape_grad

    placed = (
        P(AXES, None),
        P(AXES, None),
        P(None, AXES, None, None),
        P(AXES, None, None),
        P(AXES, None, None),
        P(AXES, None),
        P(AXES, None),
        P(),
        P(None, None, AXES),
        P(None, None, AXES),
        P(None, None, AXES),
    )
    return jax.shard_map(
        on_device,
        mesh=mesh,
        in_specs=placed,
        out_specs=(P(AXES, None), P(None, AXES)),
        check_vma=False,
    )
```

```python
import jax
import jax.numpy as jnp
from jax import lax
from jax.experimental import pallas as pl
from jax.experimental.pallas import tpu as pltpu
from jax.sharding import PartitionSpec as P

NF = 6
CORNERS = 8
AXES = ("dom", "sub")
ROWS = 16

f32 = jnp.float32
bf16 = jnp.bfloat16
i32 = jnp.int32

IN_HBM = pl.BlockSpec(memory_space=pltpu.HBM)
IN_VMEM = pl.BlockSpec(memory_space=pltpu.VMEM)


def iota(shape, dim):
    return lax.broadcasted_iota(i32, shape, dim)


def up_to(count, multiple):
    return -(-count // multiple) * multiple


def in_three(value):
    first = value.astype(bf16)
    rest = value - first.astype(f32)
    second = rest.astype(bf16)
    return first, second, (rest - second.astype(f32)).astype(bf16)


def one_hot_dot(chooser, value):
    return sum(jnp.dot(chooser, part, preferred_element_type=f32) for part in in_three(value))


def dot_nt(a, b):
    return lax.dot_general(a, b, (((1,), (1,)), ((), ())), preferred_element_type=f32)


def pair_swaps(n_dom, n_sub):
    def at(d, s):
        return d * n_sub + s

    swaps = []
    for first in (0, 1):
        pairs = []
        for s in range(n_sub):
            for d in range(first, n_dom - 1, 2):
                pairs += [(at(d, s), at(d + 1, s)), (at(d + 1, s), at(d, s))]
        swaps.append(pairs)
    for first in (0, 1):
        pairs = []
        for d in range(n_dom):
            for s in range(first, n_sub - 1, 2):
                pairs += [(at(d, s), at(d, s + 1)), (at(d, s + 1), at(d, s))]
        swaps.append(pairs)
    for index in (1, 3):
        used = {source for source, _ in swaps[index]}
        for d in range(n_dom):
            for s in range(n_sub):
                other = (d, s ^ 1) if index == 1 else (d ^ 1, s)
                if at(d, s) in used or other[0] >= n_dom or other[1] >= n_sub:
                    continue
                if at(*other) not in used:
                    swaps[index].append((at(d, s), at(*other)))
    return swaps


def face_products(elem_count, adj_rows, blocks, faces, before=None):
    def one_element(e, _):
        if before is not None:
            before(e)
        row = adj_rows[pl.ds(e, 1), :].astype(bf16)
        for k in range(NF):
            faces[k, pl.ds(e, 1), :] = jnp.dot(row, blocks[k, e], preferred_element_type=f32)
        return 0

    lax.fori_loop(0, elem_count, one_element, 0)


def fill_sends(faces, sends):
    dom_even = lax.axis_index("dom") % 2 == 0
    sub_even = lax.axis_index("sub") % 2 == 0
    sends[0][...] = jnp.where(dom_even, faces[0], faces[1])
    sends[1][...] = jnp.where(dom_even, faces[1], faces[0])
    sends[2][...] = jnp.where(sub_even, faces[2], faces[3])
    sends[3][...] = jnp.where(sub_even, faces[3], faces[2])


def sum_chooser(elem_count, n_sub, neighbor_rows, square):
    dom, sub = lax.axis_index("dom"), lax.axis_index("sub")
    device = dom * n_sub + sub
    first = device * elem_count
    square[...] = jnp.zeros(square.shape, i32)
    square[0:NF, 0:elem_count] = neighbor_rows
    by_element = square[...].T[0:ROWS, :]
    dom_odd, sub_odd = dom % 2, sub % 2
    slots = (dom_odd, 1 - dom_odd, 2 + sub_odd, 3 - sub_odd)
    offsets = (n_sub, -n_sub, 1, -1)
    columns = iota((ROWS, (NF + 4) * ROWS), 1)
    live = iota((ROWS, 1), 0) < elem_count
    total = jnp.zeros(columns.shape, f32)
    for k in range(NF):
        ids = by_element[:, k : k + 1]
        inside = (ids >= first) & (ids < first + elem_count)
        column = (k ^ 1) * ROWS + ids - first
        if k < 4:
            away = (NF + slots[k]) * ROWS + ids - first - offsets[k] * elem_count
            column = jnp.where(inside, column, away)
        column = jnp.where(live & (ids >= 0), column, -1)
        total = total + jnp.where(columns == column, 1.0, 0.0)
    return total


def corner_lanes(elem_count, node_count, corner_rows, place_row):
    width = 3 * CORNERS * elem_count
    lane = iota((CORNERS, width), 1)
    inner = lane - 3 * CORNERS * jnp.floor((lane.astype(f32) + 0.5) / (3 * CORNERS)).astype(i32)
    mine = inner - 3 * iota((CORNERS, width), 0)
    mine = (mine >= 0) & (mine < 3)
    offset = iota((elem_count, width), 1) - 3 * CORNERS * iota((elem_count, width), 0)
    spread = jnp.where((offset >= 0) & (offset < 3 * CORNERS), 1.0, 0.0).astype(bf16)
    corners = corner_rows.astype(f32)
    high = jnp.floor(corners / 128.0)
    low = corners - 128.0 * high
    nodes = 128.0 * jnp.dot(high.astype(bf16), spread, preferred_element_type=f32)
    nodes = nodes + jnp.dot(low.astype(bf16), spread, preferred_element_type=f32)
    nodes = jnp.sum(jnp.where(mine, nodes, 0.0), axis=0, keepdims=True).astype(i32)
    count = place_row.shape[1]
    found = jnp.where(iota((count, width), 0) == nodes, 1.0, 0.0).astype(bf16)
    place = jnp.broadcast_to(place_row.astype(f32), (8, count))
    owner = jnp.floor((place + 0.5) / node_count)
    slot = place - node_count * owner
    pair = jnp.where(iota((8, count), 0) == 0, owner, slot).astype(bf16)
    return jnp.dot(pair, found, preferred_element_type=f32)


def first_sweep(elem_count, n_sub, node_count, start, offdiag, neighbor, corner, place, upper,
                send_0, send_1, send_2, send_3, faces, blocks, chooser, table,
                start_v, neighbor_v, corner_v, place_v, upper_v, square, small_sem, block_sem):
    sends = (send_0, send_1, send_2, send_3)
    small = [
        pltpu.make_async_copy(source, target, small_sem.at[n])
        for n, (source, target) in enumerate(
            ((start, start_v), (neighbor, neighbor_v), (corner, corner_v), (place, place_v),
             (upper, upper_v))
        )
    ]

    def block_copy(e):
        return pltpu.make_async_copy(offdiag.at[:, e], blocks.at[:, e], block_sem.at[e])

    for copy in small:
        copy.start()
    for e in range(elem_count):
        block_copy(e).start()
    faces[...] = jnp.zeros(faces.shape, f32)
    for copy in small:
        copy.wait()
    chooser[...] = sum_chooser(elem_count, n_sub, neighbor_v[...], square)
    table[...] = jnp.zeros(table.shape, f32)
    width = 3 * CORNERS * elem_count
    table[0:8, 0:width] = corner_lanes(elem_count, node_count, corner_v[...], place_v[...][None, :])
    base = 3 * (node_count + 2)
    lane, row = iota((3, 128), 1), iota((3, 128), 0)
    last = jnp.zeros((3, 128), f32)
    for a in range(3):
        column = upper_v[a][:, node_count - 1 : node_count]
        last = last + jnp.where(lane == base + 3 * a + row, column, 0.0)
    table[2:3, 0:128] = jnp.sum(last, axis=0, keepdims=True)
    face_products(elem_count, start_v, blocks, faces, before=lambda e: block_copy(e).wait())
    fill_sends(faces, sends)


def apply_inverse(elem_count, rhs, faces, arrived, chooser, inverse, carried_v, columns):
    size = rhs.shape[1]
    terms = jnp.concatenate(
        [faces[...].reshape(NF * ROWS, size)] + [a[...] for a in arrived], axis=0
    )
    carried = one_hot_dot(chooser[...].astype(bf16), terms)
    carried_v[0:elem_count, :] = rhs[...] - carried[0:elem_count, :]
    lane = iota((size, 128), 1)
    columns[...] = jnp.zeros(columns.shape, f32)

    def one_element(e, _):
        product = inverse[e] * carried_v[pl.ds(e, 1), :]
        total = jnp.sum(product, axis=1, keepdims=True)
        columns[0:size, :] = jnp.where(lane == e, total, columns[0:size, :])
        return 0

    lax.fori_loop(0, elem_count, one_element, 0)
    return columns[...].T[0:ROWS, 0:size]


def next_sweep(elem_count, rhs, faces_in, arr_0, arr_1, arr_2, arr_3, chooser, inverse, blocks,
               send_0, send_1, send_2, send_3, faces, carried_v, columns, adj_v):
    adj_v[...] = apply_inverse(
        elem_count, rhs, faces_in, (arr_0, arr_1, arr_2, arr_3), chooser, inverse, carried_v, columns
    )
    faces[...] = jnp.zeros(faces.shape, f32)
    face_products(elem_count, adj_v, blocks, faces)
    fill_sends(faces, (send_0, send_1, send_2, send_3))


def last_sweep(elem_count, n_sub, n_dev, node_count, rhs, faces_in, arr_0, arr_1, arr_2, arr_3,
               chooser, inverse, geometry, table, adjoint, out, carried_v, columns):
    rows = apply_inverse(
        elem_count, rhs, faces_in, (arr_0, arr_1, arr_2, arr_3), chooser, inverse, carried_v, columns
    )
    adjoint[...] = rows[0:elem_count, :]
    width = 3 * CORNERS * elem_count
    slots = node_count + 2
    every = dot_nt(rows.astype(bf16), geometry[...])
    offset = iota(every.shape, 1) - 3 * CORNERS * iota(every.shape, 0)
    own = (offset >= 0) & (offset < 3 * CORNERS)
    corner = jnp.sum(jnp.where(own, every, 0.0), axis=0, keepdims=True)
    parts = in_three(corner)
    owner = table[0:1, 0:width].astype(i32)
    slot = table[1:2, 0:width].astype(i32)
    lane = iota((1, width), 1)
    third = lane - 3 * jnp.floor((lane.astype(f32) + 0.5) / 3.0).astype(i32)
    is_first, is_last = slot == 0, slot == node_count - 1
    beside = jnp.where(is_first, owner - 1, jnp.where(is_last, owner + 1, -1))
    beside_slot = jnp.where(is_first, slots - 1, 0)
    total = jnp.zeros((n_dev, 128), f32)
    for target, place in ((owner, slot + 1), (beside, beside_slot)):
        goes = iota((n_dev, width), 0) == target
        left = jnp.concatenate(
            [jnp.where(goes, part.astype(f32), 0.0).astype(bf16) for part in parts], axis=0
        )
        right = jnp.where(iota((128, width), 0) == third * slots + place, 1.0, 0.0).astype(bf16)
        summed = dot_nt(left, right)
        total = total + summed[0:n_dev] + summed[n_dev : 2 * n_dev] + summed[2 * n_dev :]
    device = lax.axis_index("dom") * n_sub + lax.axis_index("sub")
    after = iota((n_dev, 128), 0) == device + 1
    out[...] = total + jnp.where(after, table[2:3, 0:128], 0.0)


def stencil(node_count, arrived, diag, upper, lower, out, shifted):
    slots = node_count + 2
    sums = jnp.broadcast_to(jnp.sum(arrived[...], axis=0, keepdims=True), (8, 128))
    lane, row = iota((8, 128), 1), iota((8, 128), 0)

    def at(a, step):
        first = a * slots + 1 + step
        return pltpu.roll(sums, (128 - first) % 128, axis=1)[0:3, 0:node_count]

    total = jnp.zeros((3, node_count), f32)
    moved = jnp.zeros((3, node_count), f32)
    edge = jnp.zeros((8, 1), f32)
    for a in range(3):
        here = at(a, 0)
        total = total + diag[a] * here + lower[a] * at(a, 1)
        moved = moved + upper[a] * here
        coupling = jnp.sum(jnp.where(lane == 3 * slots + 3 * a + row, sums, 0.0), 1, keepdims=True)
        before = jnp.sum(jnp.where(lane == a * slots, sums, 0.0), 1, keepdims=True)
        edge = edge + coupling * before
    shifted[...] = jnp.zeros(shifted.shape, f32)
    shifted[0:3, 0:node_count] = moved
    prev = jnp.where(lane == 0, edge, pltpu.roll(shifted[...], 1, axis=1))
    out[...] = total + prev[0:3, 0:node_count]


def solution(mesh):
    n_dom, n_sub = mesh.shape["dom"], mesh.shape["sub"]
    n_dev = n_dom * n_sub
    swaps = pair_swaps(n_dom, n_sub)

    def exchange(sends):
        return [lax.ppermute(send, AXES, pairs) for send, pairs in zip(sends, swaps)]

    def on_device(
        adjoint_rhs, adjoint_start, offdiag_blocks, diag_inverse, geometry_jac, neighbor,
        corner_node, deform_place, stiff_diag, stiff_upper, stiff_lower,
    ):
        elem_count, size = adjoint_rhs.shape
        node_count = stiff_diag.shape[2]
        assert elem_count <= ROWS and n_dev <= 256 and 1 < node_count <= 256
        assert 3 * (node_count + 2) + 9 <= 128
        width = 3 * CORNERS * elem_count
        slab = jax.ShapeDtypeStruct((ROWS, size), f32)
        faces_shape = jax.ShapeDtypeStruct((NF, ROWS, size), f32)
        limit = pltpu.CompilerParams(vmem_limit_bytes=8 << 20)
        column_scratch = [
            pltpu.VMEM((ROWS, size), f32),
            pltpu.VMEM((up_to(size, 128), 128), f32),
        ]

        def fixed(body, *numbers):
            def call(*refs):
                return body(*numbers, *refs)

            return call

        *sends, faces, blocks, chooser, table = pl.pallas_call(
            fixed(first_sweep, elem_count, n_sub, node_count),
            out_shape=(
                slab, slab, slab, slab, faces_shape,
                pltpu.VMEM(offdiag_blocks.shape, bf16),
                jax.ShapeDtypeStruct((ROWS, (NF + 4) * ROWS), f32),
                jax.ShapeDtypeStruct((8, up_to(width, 128)), f32),
            ),
            in_specs=[IN_HBM] * 6,
            out_specs=(IN_VMEM,) * 8,
            scratch_shapes=[
                pltpu.VMEM((elem_count, size), f32),
                pltpu.VMEM((NF, elem_count), i32),
                pltpu.VMEM((CORNERS, elem_count), i32),
                pltpu.VMEM(deform_place.shape, i32),
                pltpu.VMEM(stiff_upper.shape, f32),
                pltpu.VMEM((128, 128), i32),
                pltpu.SemaphoreType.DMA((5,)),
                pltpu.SemaphoreType.DMA((elem_count,)),
            ],
            compiler_params=limit,
            name="first_sweep",
        )(*(pltpu.with_memory_space_constraint(a, pltpu.HBM) for a in (
            adjoint_start, offdiag_blocks, neighbor.T, corner_node.T, deform_place, stiff_upper)))
        diag_inverse, faces = lax.optimization_barrier((diag_inverse, faces))
        inverse = pltpu.with_memory_space_constraint(diag_inverse, pltpu.VMEM)
        arrived = exchange(sends)
        *sends, faces = pl.pallas_call(
            fixed(next_sweep, elem_count),
            out_shape=(slab, slab, slab, slab, faces_shape),
            in_specs=[IN_VMEM] * 9,
            out_specs=(IN_VMEM,) * 5,
            scratch_shapes=column_scratch + [pltpu.VMEM((ROWS, size), f32)],
            compiler_params=limit,
            name="next_sweep",
        )(adjoint_rhs, faces, *arrived, chooser, inverse, blocks)
        arrived = exchange(sends)
        adjoint, by_owner = pl.pallas_call(
            fixed(last_sweep, elem_count, n_sub, n_dev, node_count),
            out_shape=(
                jax.ShapeDtypeStruct((elem_count, size), f32),
                jax.ShapeDtypeStruct((n_dev, 128), f32),
            ),
            in_specs=[IN_VMEM] * 10,
            out_specs=(IN_VMEM,) * 2,
            scratch_shapes=column_scratch,
            compiler_params=limit,
            name="last_sweep",
        )(adjoint_rhs, faces, *arrived, chooser, inverse,
          geometry_jac.reshape(width, size), table)
        gathered = lax.all_to_all(by_owner, AXES, 0, 0, tiled=True)
        shape_grad = pl.pallas_call(
            fixed(stencil, node_count),
            out_shape=jax.ShapeDtypeStruct((3, node_count), f32),
            in_specs=[IN_VMEM] * 4,
            out_specs=IN_VMEM,
            scratch_shapes=[pltpu.VMEM((8, 128), f32)],
            compiler_params=limit,
            name="stencil",
        )(gathered, stiff_diag, stiff_upper, stiff_lower)
        return adjoint, shape_grad

    placed = (
        P(AXES, None),
        P(AXES, None),
        P(None, AXES, None, None),
        P(AXES, None, None),
        P(AXES, None, None),
        P(AXES, None),
        P(AXES, None),
        P(),
        P(None, None, AXES),
        P(None, None, AXES),
        P(None, None, AXES),
    )
    return jax.shard_map(
        on_device,
        mesh=mesh,
        in_specs=placed,
        out_specs=(P(AXES, None), P(None, AXES)),
        check_vma=False,
    )
```

```python
import jax
import jax.numpy as jnp
from jax import lax
from jax.experimental import pallas as pl
from jax.experimental.pallas import tpu as pltpu
from jax.sharding import PartitionSpec as P

NF = 6
CORNERS = 8
AXES = ("dom", "sub")
PAIR = 2
ROWS = 16

f32 = jnp.float32
bf16 = jnp.bfloat16
i32 = jnp.int32

IN_HBM = pl.BlockSpec(memory_space=pltpu.HBM)
IN_VMEM = pl.BlockSpec(memory_space=pltpu.VMEM)


def iota(shape, dim):
    return lax.broadcasted_iota(i32, shape, dim)


def in_hbm(array):
    return pltpu.with_memory_space_constraint(array, pltpu.HBM)


def up_to(count, multiple):
    return -(-count // multiple) * multiple


def in_three(value):
    first = value.astype(bf16)
    rest = value - first.astype(f32)
    second = rest.astype(bf16)
    return first, second, (rest - second.astype(f32)).astype(bf16)


def one_hot_dot(chooser, value):
    return sum(jnp.dot(chooser, part, preferred_element_type=f32) for part in in_three(value))


def dot_nt(a, b):
    return lax.dot_general(a, b, (((1,), (1,)), ((), ())), preferred_element_type=f32)


def grouped(count, group, one):
    def step(index, _):
        for offset in range(group):
            one(index * group + offset)
        return 0

    lax.fori_loop(0, count // group, step, 0)
    for e in range(count // group * group, count):
        one(e)


def pair_swaps(n_dom, n_sub):
    def at(d, s):
        return d * n_sub + s

    swaps = []
    for first in (0, 1):
        pairs = []
        for s in range(n_sub):
            for d in range(first, n_dom - 1, 2):
                pairs += [(at(d, s), at(d + 1, s)), (at(d + 1, s), at(d, s))]
        swaps.append(pairs)
    for first in (0, 1):
        pairs = []
        for d in range(n_dom):
            for s in range(first, n_sub - 1, 2):
                pairs += [(at(d, s), at(d, s + 1)), (at(d, s + 1), at(d, s))]
        swaps.append(pairs)
    for index in (1, 3):
        used = {source for source, _ in swaps[index]}
        for d in range(n_dom):
            for s in range(n_sub):
                other = (d, s ^ 1) if index == 1 else (d ^ 1, s)
                if at(d, s) in used or other[0] >= n_dom or other[1] >= n_sub:
                    continue
                if at(*other) not in used:
                    swaps[index].append((at(d, s), at(*other)))
    return swaps


def element_faces(e, adj_rows, blocks, faces):
    row = adj_rows[pl.ds(e, 1), :].astype(bf16)
    for k in range(NF):
        faces[k, pl.ds(e, 1), :] = jnp.dot(row, blocks[k, e], preferred_element_type=f32)


def fill_sends(faces, sends):
    dom_even = lax.axis_index("dom") % 2 == 0
    sub_even = lax.axis_index("sub") % 2 == 0
    sends[0][...] = jnp.where(dom_even, faces[0], faces[1])
    sends[1][...] = jnp.where(dom_even, faces[1], faces[0])
    sends[2][...] = jnp.where(sub_even, faces[2], faces[3])
    sends[3][...] = jnp.where(sub_even, faces[3], faces[2])


def sum_chooser(elem_count, n_sub, neighbor_rows, square):
    dom, sub = lax.axis_index("dom"), lax.axis_index("sub")
    device = dom * n_sub + sub
    first = device * elem_count
    square[...] = jnp.zeros(square.shape, i32)
    square[0:NF, 0:elem_count] = neighbor_rows
    by_element = square[...].T[0:ROWS, :]
    dom_odd, sub_odd = dom % 2, sub % 2
    slots = (dom_odd, 1 - dom_odd, 2 + sub_odd, 3 - sub_odd)
    offsets = (n_sub, -n_sub, 1, -1)
    columns = iota((ROWS, (NF + 4) * ROWS), 1)
    live = iota((ROWS, 1), 0) < elem_count
    total = jnp.zeros(columns.shape, f32)
    for k in range(NF):
        ids = by_element[:, k : k + 1]
        inside = (ids >= first) & (ids < first + elem_count)
        column = (k ^ 1) * ROWS + ids - first
        if k < 4:
            away = (NF + slots[k]) * ROWS + ids - first - offsets[k] * elem_count
            column = jnp.where(inside, column, away)
        column = jnp.where(live & (ids >= 0), column, -1)
        total = total + jnp.where(columns == column, 1.0, 0.0)
    return total


def corner_lanes(elem_count, node_count, corner_rows, place_row):
    width = 3 * CORNERS * elem_count
    lane = iota((CORNERS, width), 1)
    inner = lane - 3 * CORNERS * jnp.floor((lane.astype(f32) + 0.5) / (3 * CORNERS)).astype(i32)
    mine = inner - 3 * iota((CORNERS, width), 0)
    mine = (mine >= 0) & (mine < 3)
    offset = iota((elem_count, width), 1) - 3 * CORNERS * iota((elem_count, width), 0)
    spread = jnp.where((offset >= 0) & (offset < 3 * CORNERS), 1.0, 0.0).astype(bf16)
    corners = corner_rows.astype(f32)
    high = jnp.floor(corners / 128.0)
    low = corners - 128.0 * high
    nodes = 128.0 * jnp.dot(high.astype(bf16), spread, preferred_element_type=f32)
    nodes = nodes + jnp.dot(low.astype(bf16), spread, preferred_element_type=f32)
    nodes = jnp.sum(jnp.where(mine, nodes, 0.0), axis=0, keepdims=True).astype(i32)
    count = place_row.shape[1]
    found = jnp.where(iota((count, width), 0) == nodes, 1.0, 0.0).astype(bf16)
    place = jnp.broadcast_to(place_row.astype(f32), (8, count))
    owner = jnp.floor((place + 0.5) / node_count)
    slot = place - node_count * owner
    pair = jnp.where(iota((8, count), 0) == 0, owner, slot).astype(bf16)
    return jnp.dot(pair, found, preferred_element_type=f32)


def first_sweep(elem_count, start, offdiag, send_0, send_1, send_2, send_3, faces, blocks,
                start_v, start_sem, block_sem):
    def block_copy(index):
        held = pl.ds(index * PAIR, PAIR)
        return pltpu.make_async_copy(
            offdiag.at[:, held], blocks.at[:, held], block_sem.at[index]
        )

    start_copy = pltpu.make_async_copy(start, start_v, start_sem)
    start_copy.start()
    for index in range(elem_count // PAIR):
        block_copy(index).start()
    faces[...] = jnp.zeros(faces.shape, f32)
    start_copy.wait()

    def step(index, _):
        block_copy(index).wait()
        for offset in range(PAIR):
            element_faces(index * PAIR + offset, start_v, blocks, faces)
        return 0

    lax.fori_loop(0, elem_count // PAIR, step, 0)
    fill_sends(faces, (send_0, send_1, send_2, send_3))


def fetch_and_plan(elem_count, n_sub, node_count, inverse_hbm, neighbor, corner, place, upper,
                   after, inverse, chooser, table, square, sem):
    copy = pltpu.make_async_copy(inverse_hbm, inverse, sem)
    copy.start()
    chooser[...] = sum_chooser(elem_count, n_sub, neighbor[...], square)
    table[...] = jnp.zeros(table.shape, f32)
    width = 3 * CORNERS * elem_count
    table[0:8, 0:width] = corner_lanes(elem_count, node_count, corner[...], place[...][None, :])
    base = 3 * (node_count + 2)
    lane, row = iota((3, 128), 1), iota((3, 128), 0)
    last = jnp.zeros((3, 128), f32)
    for a in range(3):
        column = upper[a][:, node_count - 1 : node_count]
        last = last + jnp.where(lane == base + 3 * a + row, column, 0.0)
    table[2:3, 0:128] = jnp.sum(last, axis=0, keepdims=True)
    copy.wait()


def apply_inverse(elem_count, rhs, faces, arrived, chooser, inverse, carried_v, columns):
    size = rhs.shape[1]
    terms = jnp.concatenate(
        [faces[...].reshape(NF * ROWS, size)] + [a[...] for a in arrived], axis=0
    )
    carried = one_hot_dot(chooser[...].astype(bf16), terms)
    carried_v[0:elem_count, :] = rhs[...] - carried[0:elem_count, :]
    lane = iota((size, 128), 1)
    columns[...] = jnp.zeros(columns.shape, f32)

    def one_element(e, _):
        product = inverse[e] * carried_v[pl.ds(e, 1), :]
        total = jnp.sum(product, axis=1, keepdims=True)
        columns[0:size, :] = jnp.where(lane == e, total, columns[0:size, :])
        return 0

    lax.fori_loop(0, elem_count, one_element, 0)
    return columns[...].T[0:ROWS, 0:size]


def next_sweep(elem_count, rhs, faces_in, arr_0, arr_1, arr_2, arr_3, chooser, inverse, blocks,
               send_0, send_1, send_2, send_3, faces, carried_v, columns, adj_v):
    adj_v[...] = apply_inverse(
        elem_count, rhs, faces_in, (arr_0, arr_1, arr_2, arr_3), chooser, inverse, carried_v, columns
    )
    faces[...] = jnp.zeros(faces.shape, f32)
    grouped(elem_count, 4, lambda e: element_faces(e, adj_v, blocks, faces))
    fill_sends(faces, (send_0, send_1, send_2, send_3))


def last_sweep(elem_count, n_sub, n_dev, node_count, rhs, faces_in, arr_0, arr_1, arr_2, arr_3,
               chooser, inverse, geometry, table, adjoint, out, carried_v, columns):
    rows = apply_inverse(
        elem_count, rhs, faces_in, (arr_0, arr_1, arr_2, arr_3), chooser, inverse, carried_v, columns
    )
    adjoint[...] = rows[0:elem_count, :]
    width = 3 * CORNERS * elem_count
    slots = node_count + 2
    every = dot_nt(rows.astype(bf16), geometry[...])
    offset = iota(every.shape, 1) - 3 * CORNERS * iota(every.shape, 0)
    own = (offset >= 0) & (offset < 3 * CORNERS)
    corner = jnp.sum(jnp.where(own, every, 0.0), axis=0, keepdims=True)
    parts = in_three(corner)
    owner = table[0:1, 0:width].astype(i32)
    slot = table[1:2, 0:width].astype(i32)
    lane = iota((1, width), 1)
    third = lane - 3 * jnp.floor((lane.astype(f32) + 0.5) / 3.0).astype(i32)
    is_first, is_last = slot == 0, slot == node_count - 1
    beside = jnp.where(is_first, owner - 1, jnp.where(is_last, owner + 1, -1))
    beside_slot = jnp.where(is_first, slots - 1, 0)
    total = jnp.zeros((n_dev, 128), f32)
    for target, place in ((owner, slot + 1), (beside, beside_slot)):
        goes = iota((n_dev, width), 0) == target
        left = jnp.concatenate(
            [jnp.where(goes, part.astype(f32), 0.0).astype(bf16) for part in parts], axis=0
        )
        right = jnp.where(iota((128, width), 0) == third * slots + place, 1.0, 0.0).astype(bf16)
        summed = dot_nt(left, right)
        total = total + summed[0:n_dev] + summed[n_dev : 2 * n_dev] + summed[2 * n_dev :]
    device = lax.axis_index("dom") * n_sub + lax.axis_index("sub")
    after = iota((n_dev, 128), 0) == device + 1
    out[...] = total + jnp.where(after, table[2:3, 0:128], 0.0)


def stencil(node_count, arrived, diag, upper, lower, out, shifted):
    slots = node_count + 2
    sums = jnp.broadcast_to(jnp.sum(arrived[...], axis=0, keepdims=True), (8, 128))
    lane, row = iota((8, 128), 1), iota((8, 128), 0)

    def at(a, step):
        first = a * slots + 1 + step
        return pltpu.roll(sums, (128 - first) % 128, axis=1)[0:3, 0:node_count]

    total = jnp.zeros((3, node_count), f32)
    moved = jnp.zeros((3, node_count), f32)
    edge = jnp.zeros((8, 1), f32)
    for a in range(3):
        here = at(a, 0)
        total = total + diag[a] * here + lower[a] * at(a, 1)
        moved = moved + upper[a] * here
        coupling = jnp.sum(jnp.where(lane == 3 * slots + 3 * a + row, sums, 0.0), 1, keepdims=True)
        before = jnp.sum(jnp.where(lane == a * slots, sums, 0.0), 1, keepdims=True)
        edge = edge + coupling * before
    shifted[...] = jnp.zeros(shifted.shape, f32)
    shifted[0:3, 0:node_count] = moved
    prev = jnp.where(lane == 0, edge, pltpu.roll(shifted[...], 1, axis=1))
    out[...] = total + prev[0:3, 0:node_count]


def solution(mesh):
    n_dom, n_sub = mesh.shape["dom"], mesh.shape["sub"]
    n_dev = n_dom * n_sub
    swaps = pair_swaps(n_dom, n_sub)

    def exchange(sends):
        return [lax.ppermute(send, AXES, pairs) for send, pairs in zip(sends, swaps)]

    def on_device(
        adjoint_rhs, adjoint_start, offdiag_blocks, diag_inverse, geometry_jac, neighbor,
        corner_node, deform_place, stiff_diag, stiff_upper, stiff_lower,
    ):
        elem_count, size = adjoint_rhs.shape
        node_count = stiff_diag.shape[2]
        assert elem_count <= ROWS and elem_count % PAIR == 0
        assert n_dev <= 256 and 1 < node_count <= 256
        assert 3 * (node_count + 2) + 9 <= 128
        width = 3 * CORNERS * elem_count
        slab = jax.ShapeDtypeStruct((ROWS, size), f32)
        faces_shape = jax.ShapeDtypeStruct((NF, ROWS, size), f32)
        limit = pltpu.CompilerParams(vmem_limit_bytes=8 << 20)
        column_scratch = [
            pltpu.VMEM((ROWS, size), f32),
            pltpu.VMEM((up_to(size, 128), 128), f32),
        ]

        def fixed(body, *numbers):
            def call(*refs):
                return body(*numbers, *refs)

            return call

        *sends, faces, blocks = pl.pallas_call(
            fixed(first_sweep, elem_count),
            out_shape=(
                slab, slab, slab, slab, faces_shape, pltpu.VMEM(offdiag_blocks.shape, bf16),
            ),
            in_specs=[IN_HBM] * 2,
            out_specs=(IN_VMEM,) * 6,
            scratch_shapes=[
                pltpu.VMEM((elem_count, size), f32),
                pltpu.SemaphoreType.DMA,
                pltpu.SemaphoreType.DMA((elem_count // PAIR,)),
            ],
            compiler_params=limit,
            name="first_sweep",
        )(in_hbm(adjoint_start), in_hbm(offdiag_blocks))
        arrived = exchange(sends)
        inverse, chooser, table = pl.pallas_call(
            fixed(fetch_and_plan, elem_count, n_sub, node_count),
            out_shape=(
                pltpu.VMEM(diag_inverse.shape, f32),
                jax.ShapeDtypeStruct((ROWS, (NF + 4) * ROWS), f32),
                jax.ShapeDtypeStruct((8, up_to(width, 128)), f32),
            ),
            in_specs=[IN_HBM] + [IN_VMEM] * 5,
            out_specs=(IN_VMEM,) * 3,
            scratch_shapes=[pltpu.VMEM((128, 128), i32), pltpu.SemaphoreType.DMA],
            compiler_params=limit,
            cost_estimate=pl.CostEstimate(
                flops=0, bytes_accessed=4 * diag_inverse.size, transcendentals=0
            ),
            name="fetch_and_plan",
        )(in_hbm(diag_inverse), neighbor.T, corner_node.T, deform_place, stiff_upper, faces)
        *sends, faces = pl.pallas_call(
            fixed(next_sweep, elem_count),
            out_shape=(slab, slab, slab, slab, faces_shape),
            in_specs=[IN_VMEM] * 9,
            out_specs=(IN_VMEM,) * 5,
            scratch_shapes=column_scratch + [pltpu.VMEM((ROWS, size), f32)],
            compiler_params=limit,
            name="next_sweep",
        )(adjoint_rhs, faces, *arrived, chooser, inverse, blocks)
        arrived = exchange(sends)
        adjoint, by_owner = pl.pallas_call(
            fixed(last_sweep, elem_count, n_sub, n_dev, node_count),
            out_shape=(
                jax.ShapeDtypeStruct((elem_count, size), f32),
                jax.ShapeDtypeStruct((n_dev, 128), f32),
            ),
            in_specs=[IN_VMEM] * 10,
            out_specs=(IN_VMEM,) * 2,
            scratch_shapes=column_scratch,
            compiler_params=limit,
            name="last_sweep",
        )(adjoint_rhs, faces, *arrived, chooser, inverse,
          geometry_jac.reshape(width, size), table)
        gathered = lax.all_to_all(by_owner, AXES, 0, 0, tiled=True)
        shape_grad = pl.pallas_call(
            fixed(stencil, node_count),
            out_shape=jax.ShapeDtypeStruct((3, node_count), f32),
            in_specs=[IN_VMEM] * 4,
            out_specs=IN_VMEM,
            scratch_shapes=[pltpu.VMEM((8, 128), f32)],
            compiler_params=limit,
            name="stencil",
        )(gathered, stiff_diag, stiff_upper, stiff_lower)
        return adjoint, shape_grad

    placed = (
        P(AXES, None),
        P(AXES, None),
        P(None, AXES, None, None),
        P(AXES, None, None),
        P(AXES, None, None),
        P(AXES, None),
        P(AXES, None),
        P(),
        P(None, None, AXES),
        P(None, None, AXES),
        P(None, None, AXES),
    )
    return jax.shard_map(
        on_device,
        mesh=mesh,
        in_specs=placed,
        out_specs=(P(AXES, None), P(None, AXES)),
        check_vma=False,
    )
```

```python
import jax
import jax.numpy as jnp
from jax import lax
from jax.experimental import pallas as pl
from jax.experimental.pallas import tpu as pltpu
from jax.sharding import PartitionSpec as P

NF = 6
CORNERS = 8
AXES = ("dom", "sub")
PAIR = 2
AHEAD = 4
GAP_BYTES = 20_000_000
UNROLL = 4
ROWS = 16

f32 = jnp.float32
bf16 = jnp.bfloat16
i32 = jnp.int32

IN_HBM = pl.BlockSpec(memory_space=pltpu.HBM)
IN_VMEM = pl.BlockSpec(memory_space=pltpu.VMEM)


def iota(shape, dim):
    return lax.broadcasted_iota(i32, shape, dim)


def in_hbm(array):
    return pltpu.with_memory_space_constraint(array, pltpu.HBM)


def up_to(count, multiple):
    return -(-count // multiple) * multiple


def in_three(value):
    first = value.astype(bf16)
    rest = value - first.astype(f32)
    second = rest.astype(bf16)
    return first, second, (rest - second.astype(f32)).astype(bf16)


def one_hot_dot(chooser, value):
    return sum(jnp.dot(chooser, part, preferred_element_type=f32) for part in in_three(value))


def dot_nt(a, b):
    return lax.dot_general(a, b, (((1,), (1,)), ((), ())), preferred_element_type=f32)


def grouped(count, group, one):
    def step(index, _):
        for offset in range(group):
            one(index * group + offset)
        return 0

    lax.fori_loop(0, count // group, step, 0)
    for e in range(count // group * group, count):
        one(e)


def pair_swaps(n_dom, n_sub):
    def at(d, s):
        return d * n_sub + s

    swaps = []
    for first in (0, 1):
        pairs = []
        for s in range(n_sub):
            for d in range(first, n_dom - 1, 2):
                pairs += [(at(d, s), at(d + 1, s)), (at(d + 1, s), at(d, s))]
        swaps.append(pairs)
    for first in (0, 1):
        pairs = []
        for d in range(n_dom):
            for s in range(first, n_sub - 1, 2):
                pairs += [(at(d, s), at(d, s + 1)), (at(d, s + 1), at(d, s))]
        swaps.append(pairs)
    for index in (1, 3):
        used = {source for source, _ in swaps[index]}
        for d in range(n_dom):
            for s in range(n_sub):
                other = (d, s ^ 1) if index == 1 else (d ^ 1, s)
                if at(d, s) in used or other[0] >= n_dom or other[1] >= n_sub:
                    continue
                if at(*other) not in used:
                    swaps[index].append((at(d, s), at(*other)))
    return swaps


def element_faces(e, adj_rows, blocks, faces):
    row = adj_rows[pl.ds(e, 1), :].astype(bf16)
    for k in range(blocks.shape[0]):
        faces[k, pl.ds(e, 1), :] = jnp.dot(row, blocks[k, e], preferred_element_type=f32)


def send_slots():
    dom_odd, sub_odd = lax.axis_index("dom") % 2, lax.axis_index("sub") % 2
    return dom_odd, 1 - dom_odd, 2 + sub_odd, 3 - sub_odd


def fill_sends(faces, sends):
    dom_even = lax.axis_index("dom") % 2 == 0
    sub_even = lax.axis_index("sub") % 2 == 0
    sends[0][...] = jnp.where(dom_even, faces[0], faces[1])
    sends[1][...] = jnp.where(dom_even, faces[1], faces[0])
    sends[2][...] = jnp.where(sub_even, faces[2], faces[3])
    sends[3][...] = jnp.where(sub_even, faces[3], faces[2])


def sum_choosers(elem_count, n_sub, neighbor_rows, square):
    device = lax.axis_index("dom") * n_sub + lax.axis_index("sub")
    first = device * elem_count
    square[...] = jnp.zeros(square.shape, i32)
    square[0:NF, 0:elem_count] = neighbor_rows
    by_element = square[...].T[0:ROWS, :]
    slots = send_slots() + (4, 5)
    offsets = (n_sub, -n_sub, 1, -1)
    near, far = iota((ROWS, NF * ROWS), 1), iota((ROWS, 4 * ROWS), 1)
    live = iota((ROWS, 1), 0) < elem_count
    near_total, far_total = jnp.zeros(near.shape, f32), jnp.zeros(far.shape, f32)
    for k in range(NF):
        ids = by_element[:, k : k + 1]
        valid = live & (ids >= 0)
        inside = (ids >= first) & (ids < first + elem_count)
        column = jnp.where(valid & inside, slots[k ^ 1] * ROWS + ids - first, -1)
        near_total = near_total + jnp.where(near == column, 1.0, 0.0)
        if k < 4:
            column = slots[k] * ROWS + ids - first - offsets[k] * elem_count
            column = jnp.where(valid & jnp.logical_not(inside), column, -1)
            far_total = far_total + jnp.where(far == column, 1.0, 0.0)
    return near_total, far_total


def corner_lanes(elem_count, node_count, corner_rows, place_row):
    width = 3 * CORNERS * elem_count
    lane = iota((CORNERS, width), 1)
    inner = lane - 3 * CORNERS * jnp.floor((lane.astype(f32) + 0.5) / (3 * CORNERS)).astype(i32)
    mine = inner - 3 * iota((CORNERS, width), 0)
    mine = (mine >= 0) & (mine < 3)
    offset = iota((elem_count, width), 1) - 3 * CORNERS * iota((elem_count, width), 0)
    spread = jnp.where((offset >= 0) & (offset < 3 * CORNERS), 1.0, 0.0).astype(bf16)
    corners = corner_rows.astype(f32)
    high = jnp.floor(corners / 128.0)
    low = corners - 128.0 * high
    nodes = 128.0 * jnp.dot(high.astype(bf16), spread, preferred_element_type=f32)
    nodes = nodes + jnp.dot(low.astype(bf16), spread, preferred_element_type=f32)
    nodes = jnp.sum(jnp.where(mine, nodes, 0.0), axis=0, keepdims=True).astype(i32)
    count = place_row.shape[1]
    found = jnp.where(iota((count, width), 0) == nodes, 1.0, 0.0).astype(bf16)
    place = jnp.broadcast_to(place_row.astype(f32), (8, count))
    owner = jnp.floor((place + 0.5) / node_count)
    slot = place - node_count * owner
    pair = jnp.where(iota((8, count), 0) == 0, owner, slot).astype(bf16)
    return jnp.dot(pair, found, preferred_element_type=f32)


def block_copies(offdiag, first_face, blocks, sems):
    faces = pl.ds(first_face, blocks.shape[0])

    def copy(index):
        held = pl.ds(index * PAIR, PAIR)
        return pltpu.make_async_copy(offdiag.at[faces, held], blocks.at[:, held], sems.at[index])

    return copy


def start_copies(elem_count, block_copy):
    for index in range(min(AHEAD, elem_count // PAIR)):
        block_copy(index).start()


def streamed_faces(elem_count, adj_rows, block_copy, blocks, faces):
    def step(index, _):
        block_copy(index).wait()

        @pl.when(index + AHEAD < elem_count // PAIR)
        def _():
            block_copy(index + AHEAD).start()

        for offset in range(PAIR):
            element_faces(index * PAIR + offset, adj_rows, blocks, faces)
        return 0

    lax.fori_loop(0, elem_count // PAIR, step, 0)


def first_sweep(elem_count, start, offdiag, send_0, send_1, send_2, send_3, blocks,
                start_v, faces, start_sem, block_sem):
    start_copy = pltpu.make_async_copy(start, start_v, start_sem)
    block_copy = block_copies(offdiag, 0, blocks, block_sem)
    start_copy.start()
    start_copies(elem_count, block_copy)
    faces[...] = jnp.zeros(faces.shape, f32)
    start_copy.wait()
    streamed_faces(elem_count, start_v, block_copy, blocks, faces)
    fill_sends(faces, (send_0, send_1, send_2, send_3))


def local_rest(elem_count, rhs, sends, faces, near):
    terms = jnp.concatenate([send[...] for send in sends] + [faces[0], faces[1]], axis=0)
    own = one_hot_dot(near[...].astype(bf16), terms)
    return rhs[...] - own[0:elem_count, :]


def first_gap(elem_count, n_sub, offdiag, start, rhs, neighbor, send_0, send_1, send_2, send_3,
              blocks, near, far, rest, faces, square, block_sem):
    block_copy = block_copies(offdiag, 4, blocks, block_sem)
    start_copies(elem_count, block_copy)
    faces[...] = jnp.zeros(faces.shape, f32)
    near[...], far[...] = sum_choosers(elem_count, n_sub, neighbor[...], square)
    streamed_faces(elem_count, start, block_copy, blocks, faces)
    rest[...] = jnp.zeros(rest.shape, f32)
    rest[0:elem_count, :] = local_rest(
        elem_count, rhs, (send_0, send_1, send_2, send_3), faces, near
    )


def second_gap(elem_count, node_count, adj, rhs, near, blocks, corner, place, upper,
               send_0, send_1, send_2, send_3, rest, table, faces):
    faces[...] = jnp.zeros(faces.shape, f32)
    grouped(elem_count, 4, lambda e: element_faces(e, adj, blocks, faces))
    rest[...] = jnp.zeros(rest.shape, f32)
    rest[0:elem_count, :] = local_rest(
        elem_count, rhs, (send_0, send_1, send_2, send_3), faces, near
    )
    table[...] = jnp.zeros(table.shape, f32)
    width = 3 * CORNERS * elem_count
    table[0:8, 0:width] = corner_lanes(elem_count, node_count, corner[...], place[...][None, :])
    base = 3 * (node_count + 2)
    lane, row = iota((3, 128), 1), iota((3, 128), 0)
    last = jnp.zeros((3, 128), f32)
    for a in range(3):
        column = upper[a][:, node_count - 1 : node_count]
        last = last + jnp.where(lane == base + 3 * a + row, column, 0.0)
    table[2:3, 0:128] = jnp.sum(last, axis=0, keepdims=True)


def apply_inverse(elem_count, rest, arrived, far, inverse, rest_v, columns):
    size = rest.shape[1]
    terms = jnp.concatenate([a[...] for a in arrived], axis=0)
    rest_v[...] = rest[...] - one_hot_dot(far[...].astype(bf16), terms)
    lane = iota((size, 128), 1)
    columns[...] = jnp.zeros(columns.shape, f32)

    def some_elements(index, _):
        total = columns[0:size, :]
        for e in range(UNROLL):
            e = index * UNROLL + e
            product = inverse[e] * rest_v[pl.ds(e, 1), :]
            total = jnp.where(lane == e, jnp.sum(product, axis=1, keepdims=True), total)
        columns[0:size, :] = total
        return 0

    lax.fori_loop(0, elem_count // UNROLL, some_elements, 0)
    return columns[...].T[0:ROWS, 0:size]


def next_sweep(elem_count, rest, arr_0, arr_1, arr_2, arr_3, far, inverse, blocks,
               send_0, send_1, send_2, send_3, adj, rest_v, columns, faces):
    adj[...] = apply_inverse(
        elem_count, rest, (arr_0, arr_1, arr_2, arr_3), far, inverse, rest_v, columns
    )
    faces[...] = jnp.zeros(faces.shape, f32)
    grouped(elem_count, 4, lambda e: element_faces(e, adj, blocks, faces))
    fill_sends(faces, (send_0, send_1, send_2, send_3))


def last_sweep(elem_count, n_sub, n_dev, node_count, rest, arr_0, arr_1, arr_2, arr_3,
               far, inverse, geometry, table, adjoint, out, rest_v, columns):
    rows = apply_inverse(
        elem_count, rest, (arr_0, arr_1, arr_2, arr_3), far, inverse, rest_v, columns
    )
    adjoint[...] = rows[0:elem_count, :]
    width = 3 * CORNERS * elem_count
    slots = node_count + 2
    every = dot_nt(rows.astype(bf16), geometry[...])
    offset = iota(every.shape, 1) - 3 * CORNERS * iota(every.shape, 0)
    own = (offset >= 0) & (offset < 3 * CORNERS)
    corner = jnp.sum(jnp.where(own, every, 0.0), axis=0, keepdims=True)
    parts = in_three(corner)
    owner = table[0:1, 0:width].astype(i32)
    slot = table[1:2, 0:width].astype(i32)
    lane = iota((1, width), 1)
    third = lane - 3 * jnp.floor((lane.astype(f32) + 0.5) / 3.0).astype(i32)
    is_first, is_last = slot == 0, slot == node_count - 1
    beside = jnp.where(is_first, owner - 1, jnp.where(is_last, owner + 1, -1))
    beside_slot = jnp.where(is_first, slots - 1, 0)
    total = jnp.zeros((n_dev, 128), f32)
    for target, place in ((owner, slot + 1), (beside, beside_slot)):
        goes = iota((n_dev, width), 0) == target
        left = jnp.concatenate(
            [jnp.where(goes, part.astype(f32), 0.0).astype(bf16) for part in parts], axis=0
        )
        right = jnp.where(iota((128, width), 0) == third * slots + place, 1.0, 0.0).astype(bf16)
        summed = dot_nt(left, right)
        total = total + summed[0:n_dev] + summed[n_dev : 2 * n_dev] + summed[2 * n_dev :]
    device = lax.axis_index("dom") * n_sub + lax.axis_index("sub")
    after = iota((n_dev, 128), 0) == device + 1
    out[...] = total + jnp.where(after, table[2:3, 0:128], 0.0)


def stencil(node_count, arrived, diag, upper, lower, out, shifted):
    slots = node_count + 2
    sums = jnp.broadcast_to(jnp.sum(arrived[...], axis=0, keepdims=True), (8, 128))
    lane, row = iota((8, 128), 1), iota((8, 128), 0)

    def at(a, step):
        first = a * slots + 1 + step
        return pltpu.roll(sums, (128 - first) % 128, axis=1)[0:3, 0:node_count]

    total = jnp.zeros((3, node_count), f32)
    moved = jnp.zeros((3, node_count), f32)
    edge = jnp.zeros((8, 1), f32)
    for a in range(3):
        here = at(a, 0)
        total = total + diag[a] * here + lower[a] * at(a, 1)
        moved = moved + upper[a] * here
        coupling = jnp.sum(jnp.where(lane == 3 * slots + 3 * a + row, sums, 0.0), 1, keepdims=True)
        before = jnp.sum(jnp.where(lane == a * slots, sums, 0.0), 1, keepdims=True)
        edge = edge + coupling * before
    shifted[...] = jnp.zeros(shifted.shape, f32)
    shifted[0:3, 0:node_count] = moved
    prev = jnp.where(lane == 0, edge, pltpu.roll(shifted[...], 1, axis=1))
    out[...] = total + prev[0:3, 0:node_count]


def solution(mesh):
    n_dom, n_sub = mesh.shape["dom"], mesh.shape["sub"]
    n_dev = n_dom * n_sub
    swaps = pair_swaps(n_dom, n_sub)

    def exchange(sends):
        return [lax.ppermute(send, AXES, pairs) for send, pairs in zip(sends, swaps)]

    def on_device(
        adjoint_rhs, adjoint_start, offdiag_blocks, diag_inverse, geometry_jac, neighbor,
        corner_node, deform_place, stiff_diag, stiff_upper, stiff_lower,
    ):
        elem_count, size = adjoint_rhs.shape
        node_count = stiff_diag.shape[2]
        assert elem_count <= ROWS and elem_count % PAIR == 0
        assert elem_count % UNROLL == 0
        assert n_dev <= 256 and 1 < node_count <= 256
        assert 3 * (node_count + 2) + 9 <= 128
        width = 3 * CORNERS * elem_count
        slab = jax.ShapeDtypeStruct((ROWS, size), f32)
        near = jax.ShapeDtypeStruct((ROWS, NF * ROWS), f32)
        far = jax.ShapeDtypeStruct((ROWS, 4 * ROWS), f32)
        limit = pltpu.CompilerParams(vmem_limit_bytes=8 << 20)
        column_scratch = [
            pltpu.VMEM((ROWS, size), f32),
            pltpu.VMEM((up_to(size, 128), 128), f32),
        ]

        def blocks_of(faces):
            return pltpu.VMEM((faces,) + offdiag_blocks.shape[1:], bf16)

        def faces_of(faces):
            return pltpu.VMEM((faces, ROWS, size), f32)

        def fixed(body, *numbers):
            def call(*refs):
                return body(*numbers, *refs)

            return call

        offdiag = in_hbm(offdiag_blocks)
        inverse = pltpu.with_memory_space_constraint(diag_inverse, pltpu.VMEM)
        copies = elem_count // PAIR
        *sends, blocks = pl.pallas_call(
            fixed(first_sweep, elem_count),
            out_shape=(slab, slab, slab, slab, blocks_of(4)),
            in_specs=[IN_HBM] * 2,
            out_specs=(IN_VMEM,) * 5,
            scratch_shapes=[
                pltpu.VMEM((elem_count, size), f32),
                faces_of(4),
                pltpu.SemaphoreType.DMA,
                pltpu.SemaphoreType.DMA((copies,)),
            ],
            compiler_params=limit,
            name="first_sweep",
        )(in_hbm(adjoint_start), offdiag)
        arrived = exchange(sends)
        more_blocks, near, far, rest = pl.pallas_call(
            fixed(first_gap, elem_count, n_sub),
            out_shape=(blocks_of(2), near, far, slab),
            in_specs=[IN_HBM] + [IN_VMEM] * 7,
            out_specs=(IN_VMEM,) * 4,
            scratch_shapes=[
                faces_of(2), pltpu.VMEM((128, 128), i32), pltpu.SemaphoreType.DMA((copies,)),
            ],
            compiler_params=limit,
            cost_estimate=pl.CostEstimate(
                flops=0, bytes_accessed=GAP_BYTES, transcendentals=0
            ),
            name="first_gap",
        )(offdiag, adjoint_start, adjoint_rhs, neighbor.T, *sends)
        *sends, adj = pl.pallas_call(
            fixed(next_sweep, elem_count),
            out_shape=(slab,) * 5,
            in_specs=[IN_VMEM] * 8,
            out_specs=(IN_VMEM,) * 5,
            scratch_shapes=column_scratch + [faces_of(4)],
            compiler_params=limit,
            name="next_sweep",
        )(rest, *arrived, far, inverse, blocks)
        arrived = exchange(sends)
        rest, table = pl.pallas_call(
            fixed(second_gap, elem_count, node_count),
            out_shape=(slab, jax.ShapeDtypeStruct((8, up_to(width, 128)), f32)),
            in_specs=[IN_VMEM] * 11,
            out_specs=(IN_VMEM,) * 2,
            scratch_shapes=[faces_of(2)],
            compiler_params=limit,
            cost_estimate=pl.CostEstimate(
                flops=0, bytes_accessed=GAP_BYTES, transcendentals=0
            ),
            name="second_gap",
        )(adj, adjoint_rhs, near, more_blocks, corner_node.T, deform_place, stiff_upper, *sends)
        adjoint, by_owner = pl.pallas_call(
            fixed(last_sweep, elem_count, n_sub, n_dev, node_count),
            out_shape=(
                pltpu.VMEM((elem_count, size), f32),
                jax.ShapeDtypeStruct((n_dev, 128), f32),
            ),
            in_specs=[IN_VMEM] * 9,
            out_specs=(IN_VMEM,) * 2,
            scratch_shapes=column_scratch,
            compiler_params=limit,
            name="last_sweep",
        )(rest, *arrived, far, inverse, geometry_jac.reshape(width, size), table)
        gathered = lax.all_to_all(by_owner, AXES, 0, 0, tiled=True)
        shape_grad = pl.pallas_call(
            fixed(stencil, node_count),
            out_shape=jax.ShapeDtypeStruct((3, node_count), f32),
            in_specs=[IN_VMEM] * 4,
            out_specs=IN_VMEM,
            scratch_shapes=[pltpu.VMEM((8, 128), f32)],
            compiler_params=limit,
            name="stencil",
        )(gathered, stiff_diag, stiff_upper, stiff_lower)
        return adjoint, shape_grad

    placed = (
        P(AXES, None),
        P(AXES, None),
        P(None, AXES, None, None),
        P(AXES, None, None),
        P(AXES, None, None),
        P(AXES, None),
        P(AXES, None),
        P(),
        P(None, None, AXES),
        P(None, None, AXES),
        P(None, None, AXES),
    )
    return jax.shard_map(
        on_device,
        mesh=mesh,
        in_specs=placed,
        out_specs=(P(AXES, None), P(None, AXES)),
        check_vma=False,
    )
```

```python
import jax
import jax.numpy as jnp
from jax import lax
from jax.experimental import pallas as pl
from jax.experimental.pallas import tpu as pltpu
from jax.sharding import PartitionSpec as P

NF = 6
CORNERS = 8
AXES = ("dom", "sub")
PAIR = 2
AHEAD = 4
UNROLL = 12
ROWS = 16

f32 = jnp.float32
bf16 = jnp.bfloat16
i32 = jnp.int32

IN_HBM = pl.BlockSpec(memory_space=pltpu.HBM)
IN_VMEM = pl.BlockSpec(memory_space=pltpu.VMEM)


def iota(shape, dim):
    return lax.broadcasted_iota(i32, shape, dim)


def in_hbm(array):
    return pltpu.with_memory_space_constraint(array, pltpu.HBM)


def up_to(count, multiple):
    return -(-count // multiple) * multiple


def in_three(value):
    first = value.astype(bf16)
    rest = value - first.astype(f32)
    second = rest.astype(bf16)
    return first, second, (rest - second.astype(f32)).astype(bf16)


def one_hot_dot(chooser, value):
    return sum(jnp.dot(chooser, part, preferred_element_type=f32) for part in in_three(value))


def dot_nt(a, b):
    return lax.dot_general(a, b, (((1,), (1,)), ((), ())), preferred_element_type=f32)


def grouped(count, group, one):
    def step(index, _):
        for offset in range(group):
            one(index * group + offset)
        return 0

    lax.fori_loop(0, count // group, step, 0)
    for e in range(count // group * group, count):
        one(e)


def pair_swaps(n_dom, n_sub):
    def at(d, s):
        return d * n_sub + s

    swaps = []
    for first in (0, 1):
        pairs = []
        for s in range(n_sub):
            for d in range(first, n_dom - 1, 2):
                pairs += [(at(d, s), at(d + 1, s)), (at(d + 1, s), at(d, s))]
        swaps.append(pairs)
    for first in (0, 1):
        pairs = []
        for d in range(n_dom):
            for s in range(first, n_sub - 1, 2):
                pairs += [(at(d, s), at(d, s + 1)), (at(d, s + 1), at(d, s))]
        swaps.append(pairs)
    for index in (1, 3):
        used = {source for source, _ in swaps[index]}
        for d in range(n_dom):
            for s in range(n_sub):
                other = (d, s ^ 1) if index == 1 else (d ^ 1, s)
                if at(d, s) in used or other[0] >= n_dom or other[1] >= n_sub:
                    continue
                if at(*other) not in used:
                    swaps[index].append((at(d, s), at(*other)))
    return swaps


def element_faces(e, adj_rows, blocks, faces):
    row = adj_rows[pl.ds(e, 1), :].astype(bf16)
    for k in range(blocks.shape[0]):
        faces[k, pl.ds(e, 1), :] = jnp.dot(row, blocks[k, e], preferred_element_type=f32)


def send_slots():
    dom_odd, sub_odd = lax.axis_index("dom") % 2, lax.axis_index("sub") % 2
    return dom_odd, 1 - dom_odd, 2 + sub_odd, 3 - sub_odd


def fill_sends(faces, sends):
    dom_even = lax.axis_index("dom") % 2 == 0
    sub_even = lax.axis_index("sub") % 2 == 0
    sends[0][...] = jnp.where(dom_even, faces[0], faces[1])
    sends[1][...] = jnp.where(dom_even, faces[1], faces[0])
    sends[2][...] = jnp.where(sub_even, faces[2], faces[3])
    sends[3][...] = jnp.where(sub_even, faces[3], faces[2])


def sum_choosers(elem_count, n_sub, neighbor_rows, square):
    device = lax.axis_index("dom") * n_sub + lax.axis_index("sub")
    first = device * elem_count
    square[...] = jnp.zeros(square.shape, i32)
    square[0:NF, 0:elem_count] = neighbor_rows
    by_element = square[...].T[0:ROWS, :]
    slots = send_slots() + (4, 5)
    offsets = (n_sub, -n_sub, 1, -1)
    near, far = iota((ROWS, NF * ROWS), 1), iota((ROWS, 4 * ROWS), 1)
    live = iota((ROWS, 1), 0) < elem_count
    near_total, far_total = jnp.zeros(near.shape, f32), jnp.zeros(far.shape, f32)
    for k in range(NF):
        ids = by_element[:, k : k + 1]
        valid = live & (ids >= 0)
        inside = (ids >= first) & (ids < first + elem_count)
        column = jnp.where(valid & inside, slots[k ^ 1] * ROWS + ids - first, -1)
        near_total = near_total + jnp.where(near == column, 1.0, 0.0)
        if k < 4:
            column = slots[k] * ROWS + ids - first - offsets[k] * elem_count
            column = jnp.where(valid & jnp.logical_not(inside), column, -1)
            far_total = far_total + jnp.where(far == column, 1.0, 0.0)
    return near_total, far_total


def corner_lanes(elem_count, node_count, corner_rows, place_row):
    width = 3 * CORNERS * elem_count
    lane = iota((CORNERS, width), 1)
    inner = lane - 3 * CORNERS * jnp.floor((lane.astype(f32) + 0.5) / (3 * CORNERS)).astype(i32)
    mine = inner - 3 * iota((CORNERS, width), 0)
    mine = (mine >= 0) & (mine < 3)
    offset = iota((elem_count, width), 1) - 3 * CORNERS * iota((elem_count, width), 0)
    spread = jnp.where((offset >= 0) & (offset < 3 * CORNERS), 1.0, 0.0).astype(bf16)
    corners = corner_rows.astype(f32)
    high = jnp.floor(corners / 128.0)
    low = corners - 128.0 * high
    nodes = 128.0 * jnp.dot(high.astype(bf16), spread, preferred_element_type=f32)
    nodes = nodes + jnp.dot(low.astype(bf16), spread, preferred_element_type=f32)
    nodes = jnp.sum(jnp.where(mine, nodes, 0.0), axis=0, keepdims=True).astype(i32)
    count = place_row.shape[1]
    found = jnp.where(iota((count, width), 0) == nodes, 1.0, 0.0).astype(bf16)
    place = jnp.broadcast_to(place_row.astype(f32), (8, count))
    owner = jnp.floor((place + 0.5) / node_count)
    slot = place - node_count * owner
    pair = jnp.where(iota((8, count), 0) == 0, owner, slot).astype(bf16)
    return jnp.dot(pair, found, preferred_element_type=f32)


def block_copies(offdiag, first_face, blocks, sems):
    faces = pl.ds(first_face, blocks.shape[0])

    def copy(index):
        held = pl.ds(index * PAIR, PAIR)
        return pltpu.make_async_copy(offdiag.at[faces, held], blocks.at[:, held], sems.at[index])

    return copy


def start_copies(elem_count, block_copy):
    for index in range(min(AHEAD, elem_count // PAIR)):
        block_copy(index).start()


def streamed_faces(elem_count, adj_rows, block_copy, blocks, faces):
    def step(index, _):
        block_copy(index).wait()

        @pl.when(index + AHEAD < elem_count // PAIR)
        def _():
            block_copy(index + AHEAD).start()

        for offset in range(PAIR):
            element_faces(index * PAIR + offset, adj_rows, blocks, faces)
        return 0

    lax.fori_loop(0, elem_count // PAIR, step, 0)


def first_sweep(elem_count, start, offdiag, send_0, send_1, send_2, send_3, blocks,
                start_v, faces, start_sem, block_sem):
    start_copy = pltpu.make_async_copy(start, start_v, start_sem)
    block_copy = block_copies(offdiag, 0, blocks, block_sem)
    start_copy.start()
    start_copies(elem_count, block_copy)
    faces[...] = jnp.zeros(faces.shape, f32)
    start_copy.wait()
    streamed_faces(elem_count, start_v, block_copy, blocks, faces)
    fill_sends(faces, (send_0, send_1, send_2, send_3))


def local_rest(elem_count, rhs, sends, faces, near):
    terms = jnp.concatenate([send[...] for send in sends] + [faces[0], faces[1]], axis=0)
    own = one_hot_dot(near[...].astype(bf16), terms)
    return rhs[...] - own[0:elem_count, :]


def first_gap(elem_count, n_sub, node_count, offdiag, start, rhs, neighbor, corner, place, upper,
              send_0, send_1, send_2, send_3, blocks, near, far, rest, table,
              faces, square, block_sem):
    block_copy = block_copies(offdiag, 4, blocks, block_sem)
    start_copies(elem_count, block_copy)
    faces[...] = jnp.zeros(faces.shape, f32)
    near[...], far[...] = sum_choosers(elem_count, n_sub, neighbor[...], square)
    table[...] = jnp.zeros(table.shape, f32)
    width = 3 * CORNERS * elem_count
    table[0:8, 0:width] = corner_lanes(elem_count, node_count, corner[...], place[...][None, :])
    base = 3 * (node_count + 2)
    lane, row = iota((3, 128), 1), iota((3, 128), 0)
    last = jnp.zeros((3, 128), f32)
    for a in range(3):
        column = upper[a][:, node_count - 1 : node_count]
        last = last + jnp.where(lane == base + 3 * a + row, column, 0.0)
    table[2:3, 0:128] = jnp.sum(last, axis=0, keepdims=True)
    streamed_faces(elem_count, start, block_copy, blocks, faces)
    rest[...] = jnp.zeros(rest.shape, f32)
    rest[0:elem_count, :] = local_rest(
        elem_count, rhs, (send_0, send_1, send_2, send_3), faces, near
    )


def second_gap(elem_count, adj, rhs, near, blocks, send_0, send_1, send_2, send_3, rest, faces):
    faces[...] = jnp.zeros(faces.shape, f32)
    grouped(elem_count, 12, lambda e: element_faces(e, adj, blocks, faces))
    rest[...] = jnp.zeros(rest.shape, f32)
    rest[0:elem_count, :] = local_rest(
        elem_count, rhs, (send_0, send_1, send_2, send_3), faces, near
    )


def apply_inverse(elem_count, rest, arrived, far, inverse, rest_v, columns):
    size = rest.shape[1]
    terms = jnp.concatenate([a[...] for a in arrived], axis=0)
    rest_v[...] = rest[...] - one_hot_dot(far[...].astype(bf16), terms)
    lane = iota((size, 128), 1)
    columns[...] = jnp.zeros(columns.shape, f32)

    def some_elements(index, _):
        total = columns[0:size, :]
        for e in range(UNROLL):
            e = index * UNROLL + e
            product = inverse[e] * rest_v[pl.ds(e, 1), :]
            total = jnp.where(lane == e, jnp.sum(product, axis=1, keepdims=True), total)
        columns[0:size, :] = total
        return 0

    lax.fori_loop(0, elem_count // UNROLL, some_elements, 0)
    return columns[...].T[0:ROWS, 0:size]


def next_sweep(elem_count, rest, arr_0, arr_1, arr_2, arr_3, far, inverse, blocks,
               send_0, send_1, send_2, send_3, adj, rest_v, columns, faces):
    adj[...] = apply_inverse(
        elem_count, rest, (arr_0, arr_1, arr_2, arr_3), far, inverse, rest_v, columns
    )
    faces[...] = jnp.zeros(faces.shape, f32)
    grouped(elem_count, 12, lambda e: element_faces(e, adj, blocks, faces))
    fill_sends(faces, (send_0, send_1, send_2, send_3))


def last_sweep(elem_count, n_sub, n_dev, node_count, rest, arr_0, arr_1, arr_2, arr_3,
               far, inverse, geometry, table, adjoint, out, rest_v, columns):
    rows = apply_inverse(
        elem_count, rest, (arr_0, arr_1, arr_2, arr_3), far, inverse, rest_v, columns
    )
    adjoint[...] = rows[0:elem_count, :]
    width = 3 * CORNERS * elem_count
    slots = node_count + 2
    every = dot_nt(rows.astype(bf16), geometry[...])
    offset = iota(every.shape, 1) - 3 * CORNERS * iota(every.shape, 0)
    own = (offset >= 0) & (offset < 3 * CORNERS)
    corner = jnp.sum(jnp.where(own, every, 0.0), axis=0, keepdims=True)
    parts = in_three(corner)
    owner = table[0:1, 0:width].astype(i32)
    slot = table[1:2, 0:width].astype(i32)
    lane = iota((1, width), 1)
    third = lane - 3 * jnp.floor((lane.astype(f32) + 0.5) / 3.0).astype(i32)
    is_first, is_last = slot == 0, slot == node_count - 1
    beside = jnp.where(is_first, owner - 1, jnp.where(is_last, owner + 1, -1))
    beside_slot = jnp.where(is_first, slots - 1, 0)
    total = jnp.zeros((n_dev, 128), f32)
    for target, place in ((owner, slot + 1), (beside, beside_slot)):
        goes = iota((n_dev, width), 0) == target
        left = jnp.concatenate(
            [jnp.where(goes, part.astype(f32), 0.0).astype(bf16) for part in parts], axis=0
        )
        right = jnp.where(iota((128, width), 0) == third * slots + place, 1.0, 0.0).astype(bf16)
        summed = dot_nt(left, right)
        total = total + summed[0:n_dev] + summed[n_dev : 2 * n_dev] + summed[2 * n_dev :]
    device = lax.axis_index("dom") * n_sub + lax.axis_index("sub")
    after = iota((n_dev, 128), 0) == device + 1
    out[...] = total + jnp.where(after, table[2:3, 0:128], 0.0)


def stencil(node_count, arrived, diag, upper, lower, out, shifted):
    slots = node_count + 2
    sums = jnp.broadcast_to(jnp.sum(arrived[...], axis=0, keepdims=True), (8, 128))
    lane, row = iota((8, 128), 1), iota((8, 128), 0)

    def at(a, step):
        first = a * slots + 1 + step
        return pltpu.roll(sums, (128 - first) % 128, axis=1)[0:3, 0:node_count]

    total = jnp.zeros((3, node_count), f32)
    moved = jnp.zeros((3, node_count), f32)
    edge = jnp.zeros((8, 1), f32)
    for a in range(3):
        here = at(a, 0)
        total = total + diag[a] * here + lower[a] * at(a, 1)
        moved = moved + upper[a] * here
        coupling = jnp.sum(jnp.where(lane == 3 * slots + 3 * a + row, sums, 0.0), 1, keepdims=True)
        before = jnp.sum(jnp.where(lane == a * slots, sums, 0.0), 1, keepdims=True)
        edge = edge + coupling * before
    shifted[...] = jnp.zeros(shifted.shape, f32)
    shifted[0:3, 0:node_count] = moved
    prev = jnp.where(lane == 0, edge, pltpu.roll(shifted[...], 1, axis=1))
    out[...] = total + prev[0:3, 0:node_count]


def solution(mesh):
    n_dom, n_sub = mesh.shape["dom"], mesh.shape["sub"]
    n_dev = n_dom * n_sub
    swaps = pair_swaps(n_dom, n_sub)

    def exchange(sends):
        return [lax.ppermute(send, AXES, pairs) for send, pairs in zip(sends, swaps)]

    def on_device(
        adjoint_rhs, adjoint_start, offdiag_blocks, diag_inverse, geometry_jac, neighbor,
        corner_node, deform_place, stiff_diag, stiff_upper, stiff_lower,
    ):
        elem_count, size = adjoint_rhs.shape
        node_count = stiff_diag.shape[2]
        assert elem_count <= ROWS and elem_count % PAIR == 0
        assert elem_count % UNROLL == 0
        assert n_dev <= 256 and 1 < node_count <= 256
        assert 3 * (node_count + 2) + 9 <= 128
        width = 3 * CORNERS * elem_count
        slab = jax.ShapeDtypeStruct((ROWS, size), f32)
        near = jax.ShapeDtypeStruct((ROWS, NF * ROWS), f32)
        far = jax.ShapeDtypeStruct((ROWS, 4 * ROWS), f32)
        limit = pltpu.CompilerParams(vmem_limit_bytes=8 << 20)
        column_scratch = [
            pltpu.VMEM((ROWS, size), f32),
            pltpu.VMEM((up_to(size, 128), 128), f32),
        ]

        def blocks_of(faces):
            return pltpu.VMEM((faces,) + offdiag_blocks.shape[1:], bf16)

        def faces_of(faces):
            return pltpu.VMEM((faces, ROWS, size), f32)

        def fixed(body, *numbers):
            def call(*refs):
                return body(*numbers, *refs)

            return call

        offdiag = in_hbm(offdiag_blocks)
        inverse = pltpu.with_memory_space_constraint(diag_inverse, pltpu.VMEM)
        copies = elem_count // PAIR
        *sends, blocks = pl.pallas_call(
            fixed(first_sweep, elem_count),
            out_shape=(slab, slab, slab, slab, blocks_of(4)),
            in_specs=[IN_HBM] * 2,
            out_specs=(IN_VMEM,) * 5,
            scratch_shapes=[
                pltpu.VMEM((elem_count, size), f32),
                faces_of(4),
                pltpu.SemaphoreType.DMA,
                pltpu.SemaphoreType.DMA((copies,)),
            ],
            compiler_params=limit,
            name="first_sweep",
        )(in_hbm(adjoint_start), offdiag)
        arrived = exchange(sends)
        more_blocks, near, far, rest, table = pl.pallas_call(
            fixed(first_gap, elem_count, n_sub, node_count),
            out_shape=(
                blocks_of(2), near, far, slab,
                jax.ShapeDtypeStruct((8, up_to(width, 128)), f32),
            ),
            in_specs=[IN_HBM] + [IN_VMEM] * 10,
            out_specs=(IN_VMEM,) * 5,
            scratch_shapes=[
                faces_of(2), pltpu.VMEM((128, 128), i32), pltpu.SemaphoreType.DMA((copies,)),
            ],
            compiler_params=limit,
            cost_estimate=pl.CostEstimate(
                flops=0, bytes_accessed=2 * elem_count * size * size * 2, transcendentals=0
            ),
            name="first_gap",
        )(offdiag, adjoint_start, adjoint_rhs, neighbor.T, corner_node.T, deform_place, stiff_upper,
          *sends)
        *sends, adj = pl.pallas_call(
            fixed(next_sweep, elem_count),
            out_shape=(slab,) * 5,
            in_specs=[IN_VMEM] * 8,
            out_specs=(IN_VMEM,) * 5,
            scratch_shapes=column_scratch + [faces_of(4)],
            compiler_params=limit,
            name="next_sweep",
        )(rest, *arrived, far, inverse, blocks)
        arrived = exchange(sends)
        rest = pl.pallas_call(
            fixed(second_gap, elem_count),
            out_shape=slab,
            in_specs=[IN_VMEM] * 8,
            out_specs=IN_VMEM,
            scratch_shapes=[faces_of(2)],
            compiler_params=limit,
            cost_estimate=pl.CostEstimate(
                flops=0, bytes_accessed=2 * elem_count * size * size * 2, transcendentals=0
            ),
            name="second_gap",
        )(adj, adjoint_rhs, near, more_blocks, *sends)
        adjoint, by_owner = pl.pallas_call(
            fixed(last_sweep, elem_count, n_sub, n_dev, node_count),
            out_shape=(
                jax.ShapeDtypeStruct((elem_count, size), f32),
                pltpu.VMEM((n_dev, 128), f32),
            ),
            in_specs=[IN_VMEM] * 9,
            out_specs=(IN_VMEM,) * 2,
            scratch_shapes=column_scratch,
            compiler_params=limit,
            name="last_sweep",
        )(rest, *arrived, far, inverse, geometry_jac.reshape(width, size), table)
        gathered = lax.all_to_all(by_owner, AXES, 0, 0, tiled=True)
        shape_grad = pl.pallas_call(
            fixed(stencil, node_count),
            out_shape=jax.ShapeDtypeStruct((3, node_count), f32),
            in_specs=[IN_VMEM] * 4,
            out_specs=IN_VMEM,
            scratch_shapes=[pltpu.VMEM((8, 128), f32)],
            compiler_params=limit,
            name="stencil",
        )(gathered, stiff_diag, stiff_upper, stiff_lower)
        return adjoint, shape_grad

    placed = (
        P(AXES, None),
        P(AXES, None),
        P(None, AXES, None, None),
        P(AXES, None, None),
        P(AXES, None, None),
        P(AXES, None),
        P(AXES, None),
        P(),
        P(None, None, AXES),
        P(None, None, AXES),
        P(None, None, AXES),
    )
    return jax.shard_map(
        on_device,
        mesh=mesh,
        in_specs=placed,
        out_specs=(P(AXES, None), P(None, AXES)),
        check_vma=False,
    )
```

```python
import jax
import jax.numpy as jnp
from jax import lax
from jax.experimental import pallas as pl
from jax.experimental.pallas import tpu as pltpu
from jax.sharding import PartitionSpec as P

NF = 6
CORNERS = 8
AXES = ("dom", "sub")
PAIR = 2
SWEEP_AHEAD = 4
GAP_AHEAD = 6
UNROLL = 12
ROWS = 16

f32 = jnp.float32
bf16 = jnp.bfloat16
i32 = jnp.int32

IN_HBM = pl.BlockSpec(memory_space=pltpu.HBM)
IN_VMEM = pl.BlockSpec(memory_space=pltpu.VMEM)


def iota(shape, dim):
    return lax.broadcasted_iota(i32, shape, dim)


def in_hbm(array):
    return pltpu.with_memory_space_constraint(array, pltpu.HBM)


def up_to(count, multiple):
    return -(-count // multiple) * multiple


def in_three(value):
    first = value.astype(bf16)
    rest = value - first.astype(f32)
    second = rest.astype(bf16)
    return first, second, (rest - second.astype(f32)).astype(bf16)


def one_hot_dot(chooser, value):
    return sum(jnp.dot(chooser, part, preferred_element_type=f32) for part in in_three(value))


def dot_nt(a, b):
    return lax.dot_general(a, b, (((1,), (1,)), ((), ())), preferred_element_type=f32)


def grouped(count, group, one):
    def step(index, _):
        for offset in range(group):
            one(index * group + offset)
        return 0

    lax.fori_loop(0, count // group, step, 0)
    for e in range(count // group * group, count):
        one(e)


def pair_swaps(n_dom, n_sub):
    def at(d, s):
        return d * n_sub + s

    swaps = []
    for first in (0, 1):
        pairs = []
        for s in range(n_sub):
            for d in range(first, n_dom - 1, 2):
                pairs += [(at(d, s), at(d + 1, s)), (at(d + 1, s), at(d, s))]
        swaps.append(pairs)
    for first in (0, 1):
        pairs = []
        for d in range(n_dom):
            for s in range(first, n_sub - 1, 2):
                pairs += [(at(d, s), at(d, s + 1)), (at(d, s + 1), at(d, s))]
        swaps.append(pairs)
    for index in (1, 3):
        used = {source for source, _ in swaps[index]}
        for d in range(n_dom):
            for s in range(n_sub):
                other = (d, s ^ 1) if index == 1 else (d ^ 1, s)
                if at(d, s) in used or other[0] >= n_dom or other[1] >= n_sub:
                    continue
                if at(*other) not in used:
                    swaps[index].append((at(d, s), at(*other)))
    return swaps


def element_faces(e, adj_rows, blocks, faces):
    row = adj_rows[pl.ds(e, 1), :].astype(bf16)
    for k in range(blocks.shape[0]):
        faces[k, pl.ds(e, 1), :] = jnp.dot(row, blocks[k, e], preferred_element_type=f32)


def send_slots():
    dom_odd, sub_odd = lax.axis_index("dom") % 2, lax.axis_index("sub") % 2
    return dom_odd, 1 - dom_odd, 2 + sub_odd, 3 - sub_odd


def fill_sends(faces, sends):
    dom_even = lax.axis_index("dom") % 2 == 0
    sub_even = lax.axis_index("sub") % 2 == 0
    sends[0][...] = jnp.where(dom_even, faces[0], faces[1])
    sends[1][...] = jnp.where(dom_even, faces[1], faces[0])
    sends[2][...] = jnp.where(sub_even, faces[2], faces[3])
    sends[3][...] = jnp.where(sub_even, faces[3], faces[2])


def sum_choosers(elem_count, n_sub, neighbor_rows, square):
    device = lax.axis_index("dom") * n_sub + lax.axis_index("sub")
    first = device * elem_count
    square[...] = jnp.zeros(square.shape, i32)
    square[0:NF, 0:elem_count] = neighbor_rows
    by_element = square[...].T[0:ROWS, :]
    slots = send_slots() + (4, 5)
    offsets = (n_sub, -n_sub, 1, -1)
    near, far = iota((ROWS, NF * ROWS), 1), iota((ROWS, 4 * ROWS), 1)
    live = iota((ROWS, 1), 0) < elem_count
    near_total, far_total = jnp.zeros(near.shape, f32), jnp.zeros(far.shape, f32)
    for k in range(NF):
        ids = by_element[:, k : k + 1]
        valid = live & (ids >= 0)
        inside = (ids >= first) & (ids < first + elem_count)
        column = jnp.where(valid & inside, slots[k ^ 1] * ROWS + ids - first, -1)
        near_total = near_total + jnp.where(near == column, 1.0, 0.0)
        if k < 4:
            column = slots[k] * ROWS + ids - first - offsets[k] * elem_count
            column = jnp.where(valid & jnp.logical_not(inside), column, -1)
            far_total = far_total + jnp.where(far == column, 1.0, 0.0)
    return near_total, far_total


def corner_lanes(elem_count, node_count, corner_rows, place_row):
    width = 3 * CORNERS * elem_count
    lane = iota((CORNERS, width), 1)
    inner = lane - 3 * CORNERS * jnp.floor((lane.astype(f32) + 0.5) / (3 * CORNERS)).astype(i32)
    mine = inner - 3 * iota((CORNERS, width), 0)
    mine = (mine >= 0) & (mine < 3)
    offset = iota((elem_count, width), 1) - 3 * CORNERS * iota((elem_count, width), 0)
    spread = jnp.where((offset >= 0) & (offset < 3 * CORNERS), 1.0, 0.0).astype(bf16)
    corners = corner_rows.astype(f32)
    high = jnp.floor(corners / 128.0)
    low = corners - 128.0 * high
    nodes = 128.0 * jnp.dot(high.astype(bf16), spread, preferred_element_type=f32)
    nodes = nodes + jnp.dot(low.astype(bf16), spread, preferred_element_type=f32)
    nodes = jnp.sum(jnp.where(mine, nodes, 0.0), axis=0, keepdims=True).astype(i32)
    count = place_row.shape[1]
    found = jnp.where(iota((count, width), 0) == nodes, 1.0, 0.0).astype(bf16)
    place = jnp.broadcast_to(place_row.astype(f32), (8, count))
    owner = jnp.floor((place + 0.5) / node_count)
    slot = place - node_count * owner
    pair = jnp.where(iota((8, count), 0) == 0, owner, slot).astype(bf16)
    return jnp.dot(pair, found, preferred_element_type=f32)


def block_copies(offdiag, first_face, blocks, sems):
    faces = pl.ds(first_face, blocks.shape[0])

    def copy(index):
        held = pl.ds(index * PAIR, PAIR)
        return pltpu.make_async_copy(offdiag.at[faces, held], blocks.at[:, held], sems.at[index])

    return copy


def start_copies(elem_count, block_copy, ahead):
    for index in range(min(ahead, elem_count // PAIR)):
        block_copy(index).start()


def streamed_faces(elem_count, adj_rows, block_copy, blocks, faces, ahead):
    def step(index, _):
        block_copy(index).wait()

        @pl.when(index + ahead < elem_count // PAIR)
        def _():
            block_copy(index + ahead).start()

        for offset in range(PAIR):
            element_faces(index * PAIR + offset, adj_rows, blocks, faces)
        return 0

    lax.fori_loop(0, elem_count // PAIR, step, 0)


def first_sweep(elem_count, start, offdiag, send_0, send_1, send_2, send_3, blocks,
                start_v, faces, start_sem, block_sem):
    start_copy = pltpu.make_async_copy(start, start_v, start_sem)
    block_copy = block_copies(offdiag, 0, blocks, block_sem)
    start_copy.start()
    start_copies(elem_count, block_copy, SWEEP_AHEAD)
    faces[...] = jnp.zeros(faces.shape, f32)
    start_copy.wait()
    streamed_faces(elem_count, start_v, block_copy, blocks, faces, SWEEP_AHEAD)
    fill_sends(faces, (send_0, send_1, send_2, send_3))


def local_rest(elem_count, rhs, sends, faces, near):
    terms = jnp.concatenate([send[...] for send in sends] + [faces[0], faces[1]], axis=0)
    own = one_hot_dot(near[...].astype(bf16), terms)
    return rhs[...] - own[0:elem_count, :]


def first_gap(elem_count, n_sub, node_count, offdiag, start, rhs, neighbor, corner, place, upper,
              send_0, send_1, send_2, send_3, blocks, near, far, rest, table,
              faces, square, block_sem):
    block_copy = block_copies(offdiag, 4, blocks, block_sem)
    start_copies(elem_count, block_copy, GAP_AHEAD)
    faces[...] = jnp.zeros(faces.shape, f32)
    near[...], far[...] = sum_choosers(elem_count, n_sub, neighbor[...], square)
    table[...] = jnp.zeros(table.shape, f32)
    width = 3 * CORNERS * elem_count
    table[0:8, 0:width] = corner_lanes(elem_count, node_count, corner[...], place[...][None, :])
    base = 3 * (node_count + 2)
    lane, row = iota((3, 128), 1), iota((3, 128), 0)
    last = jnp.zeros((3, 128), f32)
    for a in range(3):
        column = upper[a][:, node_count - 1 : node_count]
        last = last + jnp.where(lane == base + 3 * a + row, column, 0.0)
    table[2:3, 0:128] = jnp.sum(last, axis=0, keepdims=True)
    streamed_faces(elem_count, start, block_copy, blocks, faces, GAP_AHEAD)
    rest[...] = jnp.zeros(rest.shape, f32)
    rest[0:elem_count, :] = local_rest(
        elem_count, rhs, (send_0, send_1, send_2, send_3), faces, near
    )


def second_gap(elem_count, adj, rhs, near, blocks, send_0, send_1, send_2, send_3, rest, faces):
    faces[...] = jnp.zeros(faces.shape, f32)
    grouped(elem_count, 12, lambda e: element_faces(e, adj, blocks, faces))
    rest[...] = jnp.zeros(rest.shape, f32)
    rest[0:elem_count, :] = local_rest(
        elem_count, rhs, (send_0, send_1, send_2, send_3), faces, near
    )


def apply_inverse(elem_count, rest, arrived, far, inverse, rest_v, columns):
    size = rest.shape[1]
    terms = jnp.concatenate([a[...] for a in arrived], axis=0)
    rest_v[...] = rest[...] - one_hot_dot(far[...].astype(bf16), terms)
    lane = iota((size, 128), 1)
    columns[...] = jnp.zeros(columns.shape, f32)

    def some_elements(index, _):
        total = columns[0:size, :]
        for e in range(UNROLL):
            e = index * UNROLL + e
            product = inverse[e] * rest_v[pl.ds(e, 1), :]
            total = jnp.where(lane == e, jnp.sum(product, axis=1, keepdims=True), total)
        columns[0:size, :] = total
        return 0

    lax.fori_loop(0, elem_count // UNROLL, some_elements, 0)
    return columns[...].T[0:ROWS, 0:size]


def next_sweep(elem_count, rest, arr_0, arr_1, arr_2, arr_3, far, inverse, blocks,
               send_0, send_1, send_2, send_3, adj, rest_v, columns, faces):
    adj[...] = apply_inverse(
        elem_count, rest, (arr_0, arr_1, arr_2, arr_3), far, inverse, rest_v, columns
    )
    faces[...] = jnp.zeros(faces.shape, f32)
    grouped(elem_count, 12, lambda e: element_faces(e, adj, blocks, faces))
    fill_sends(faces, (send_0, send_1, send_2, send_3))


def last_sweep(elem_count, n_sub, n_dev, node_count, rest, arr_0, arr_1, arr_2, arr_3,
               far, inverse, geometry, table, adjoint, out, rest_v, columns):
    rows = apply_inverse(
        elem_count, rest, (arr_0, arr_1, arr_2, arr_3), far, inverse, rest_v, columns
    )
    adjoint[...] = rows[0:elem_count, :]
    width = 3 * CORNERS * elem_count
    slots = node_count + 2
    every = dot_nt(rows.astype(bf16), geometry[...])
    offset = iota(every.shape, 1) - 3 * CORNERS * iota(every.shape, 0)
    own = (offset >= 0) & (offset < 3 * CORNERS)
    corner = jnp.sum(jnp.where(own, every, 0.0), axis=0, keepdims=True)
    parts = in_three(corner)
    owner = table[0:1, 0:width].astype(i32)
    slot = table[1:2, 0:width].astype(i32)
    lane = iota((1, width), 1)
    third = lane - 3 * jnp.floor((lane.astype(f32) + 0.5) / 3.0).astype(i32)
    is_first, is_last = slot == 0, slot == node_count - 1
    beside = jnp.where(is_first, owner - 1, jnp.where(is_last, owner + 1, -1))
    beside_slot = jnp.where(is_first, slots - 1, 0)
    total = jnp.zeros((n_dev, 128), f32)
    for target, place in ((owner, slot + 1), (beside, beside_slot)):
        goes = iota((n_dev, width), 0) == target
        left = jnp.concatenate(
            [jnp.where(goes, part.astype(f32), 0.0).astype(bf16) for part in parts], axis=0
        )
        right = jnp.where(iota((128, width), 0) == third * slots + place, 1.0, 0.0).astype(bf16)
        summed = dot_nt(left, right)
        total = total + summed[0:n_dev] + summed[n_dev : 2 * n_dev] + summed[2 * n_dev :]
    device = lax.axis_index("dom") * n_sub + lax.axis_index("sub")
    after = iota((n_dev, 128), 0) == device + 1
    out[...] = total + jnp.where(after, table[2:3, 0:128], 0.0)


def stencil(node_count, arrived, diag, upper, lower, out, shifted):
    slots = node_count + 2
    sums = jnp.broadcast_to(jnp.sum(arrived[...], axis=0, keepdims=True), (8, 128))
    lane, row = iota((8, 128), 1), iota((8, 128), 0)

    def at(a, step):
        first = a * slots + 1 + step
        return pltpu.roll(sums, (128 - first) % 128, axis=1)[0:3, 0:node_count]

    total = jnp.zeros((3, node_count), f32)
    moved = jnp.zeros((3, node_count), f32)
    edge = jnp.zeros((8, 1), f32)
    for a in range(3):
        here = at(a, 0)
        total = total + diag[a] * here + lower[a] * at(a, 1)
        moved = moved + upper[a] * here
        coupling = jnp.sum(jnp.where(lane == 3 * slots + 3 * a + row, sums, 0.0), 1, keepdims=True)
        before = jnp.sum(jnp.where(lane == a * slots, sums, 0.0), 1, keepdims=True)
        edge = edge + coupling * before
    shifted[...] = jnp.zeros(shifted.shape, f32)
    shifted[0:3, 0:node_count] = moved
    prev = jnp.where(lane == 0, edge, pltpu.roll(shifted[...], 1, axis=1))
    out[...] = total + prev[0:3, 0:node_count]


def solution(mesh):
    n_dom, n_sub = mesh.shape["dom"], mesh.shape["sub"]
    n_dev = n_dom * n_sub
    swaps = pair_swaps(n_dom, n_sub)

    def exchange(sends):
        return [lax.ppermute(send, AXES, pairs) for send, pairs in zip(sends, swaps)]

    def on_device(
        adjoint_rhs, adjoint_start, offdiag_blocks, diag_inverse, geometry_jac, neighbor,
        corner_node, deform_place, stiff_diag, stiff_upper, stiff_lower,
    ):
        elem_count, size = adjoint_rhs.shape
        node_count = stiff_diag.shape[2]
        assert elem_count <= ROWS and elem_count % PAIR == 0
        assert elem_count % UNROLL == 0
        assert n_dev <= 256 and 1 < node_count <= 256
        assert 3 * (node_count + 2) + 9 <= 128
        width = 3 * CORNERS * elem_count
        slab = jax.ShapeDtypeStruct((ROWS, size), f32)
        near = jax.ShapeDtypeStruct((ROWS, NF * ROWS), f32)
        far = jax.ShapeDtypeStruct((ROWS, 4 * ROWS), f32)
        limit = pltpu.CompilerParams(vmem_limit_bytes=8 << 20)
        column_scratch = [
            pltpu.VMEM((ROWS, size), f32),
            pltpu.VMEM((up_to(size, 128), 128), f32),
        ]

        def blocks_of(faces):
            return pltpu.VMEM((faces,) + offdiag_blocks.shape[1:], bf16)

        def faces_of(faces):
            return pltpu.VMEM((faces, ROWS, size), f32)

        def fixed(body, *numbers):
            def call(*refs):
                return body(*numbers, *refs)

            return call

        offdiag = in_hbm(offdiag_blocks)
        inverse = pltpu.with_memory_space_constraint(diag_inverse, pltpu.VMEM)
        copies = elem_count // PAIR
        *sends, blocks = pl.pallas_call(
            fixed(first_sweep, elem_count),
            out_shape=(slab, slab, slab, slab, blocks_of(4)),
            in_specs=[IN_HBM] * 2,
            out_specs=(IN_VMEM,) * 5,
            scratch_shapes=[
                pltpu.VMEM((elem_count, size), f32),
                faces_of(4),
                pltpu.SemaphoreType.DMA,
                pltpu.SemaphoreType.DMA((copies,)),
            ],
            compiler_params=limit,
            name="first_sweep",
        )(in_hbm(adjoint_start), offdiag)
        arrived = exchange(sends)
        more_blocks, near, far, rest, table = pl.pallas_call(
            fixed(first_gap, elem_count, n_sub, node_count),
            out_shape=(
                blocks_of(2), near, far, slab,
                jax.ShapeDtypeStruct((8, up_to(width, 128)), f32),
            ),
            in_specs=[IN_HBM] + [IN_VMEM] * 10,
            out_specs=(IN_VMEM,) * 5,
            scratch_shapes=[
                faces_of(2), pltpu.VMEM((128, 128), i32), pltpu.SemaphoreType.DMA((copies,)),
            ],
            compiler_params=limit,
            cost_estimate=pl.CostEstimate(
                flops=0, bytes_accessed=2 * elem_count * size * size * 2, transcendentals=0
            ),
            name="first_gap",
        )(offdiag, adjoint_start, adjoint_rhs, neighbor.T, corner_node.T, deform_place, stiff_upper,
          *sends)
        *sends, adj = pl.pallas_call(
            fixed(next_sweep, elem_count),
            out_shape=(slab,) * 5,
            in_specs=[IN_VMEM] * 8,
            out_specs=(IN_VMEM,) * 5,
            scratch_shapes=column_scratch + [faces_of(4)],
            compiler_params=limit,
            name="next_sweep",
        )(rest, *arrived, far, inverse, blocks)
        arrived = exchange(sends)
        rest = pl.pallas_call(
            fixed(second_gap, elem_count),
            out_shape=slab,
            in_specs=[IN_VMEM] * 8,
            out_specs=IN_VMEM,
            scratch_shapes=[faces_of(2)],
            compiler_params=limit,
            cost_estimate=pl.CostEstimate(
                flops=0, bytes_accessed=2 * elem_count * size * size * 2, transcendentals=0
            ),
            name="second_gap",
        )(adj, adjoint_rhs, near, more_blocks, *sends)
        adjoint, by_owner = pl.pallas_call(
            fixed(last_sweep, elem_count, n_sub, n_dev, node_count),
            out_shape=(
                jax.ShapeDtypeStruct((elem_count, size), f32),
                pltpu.VMEM((n_dev, 128), f32),
            ),
            in_specs=[IN_VMEM] * 9,
            out_specs=(IN_VMEM,) * 2,
            scratch_shapes=column_scratch,
            compiler_params=limit,
            name="last_sweep",
        )(rest, *arrived, far, inverse, geometry_jac.reshape(width, size), table)
        gathered = lax.all_to_all(by_owner, AXES, 0, 0, tiled=True)
        shape_grad = pl.pallas_call(
            fixed(stencil, node_count),
            out_shape=jax.ShapeDtypeStruct((3, node_count), f32),
            in_specs=[IN_VMEM] * 4,
            out_specs=IN_VMEM,
            scratch_shapes=[pltpu.VMEM((8, 128), f32)],
            compiler_params=limit,
            name="stencil",
        )(gathered, stiff_diag, stiff_upper, stiff_lower)
        return adjoint, shape_grad

    placed = (
        P(AXES, None),
        P(AXES, None),
        P(None, AXES, None, None),
        P(AXES, None, None),
        P(AXES, None, None),
        P(AXES, None),
        P(AXES, None),
        P(),
        P(None, None, AXES),
        P(None, None, AXES),
        P(None, None, AXES),
    )
    return jax.shard_map(
        on_device,
        mesh=mesh,
        in_specs=placed,
        out_specs=(P(AXES, None), P(None, AXES)),
        check_vma=False,
    )
```
